768 devices in a mesh: seq: 16 (over y, core), chan: 48 (over z, x).
Axes of the slice: x: 4, y: 8, z: 12, core: 2. Of those that a mesh axis runs over, the one named last changes fastest.
Arguments:
- queries: bfloat16 [48, 2048, 4096], P('chan', 'seq'), may hold values from -256 to 256
- keys: bfloat16 [48, 2048, 1024], P('chan', 'seq'), may hold values from -6 to 6
- values: bfloat16 [48, 2048, 1024], P('chan', 'seq'), may hold values from -6 to 6
- doc_lengths: int32 [48, 16], P('chan'), may hold values from 1 to 256, 2048 in all within a row
- rank_in: bfloat16 [4096, 256], replicated, may hold values from -0.09375 to 0.09375
- bc_weight: bfloat16 [4096, 32], replicated, may hold values from -0.09375 to 0.09375
- rank_out: bfloat16 [256, 4096], replicated, may hold values from -0.375 to 0.375
- dt_bias: float32 [4096], replicated, may hold values from -8 to -6
- a_log: float32 [4096, 16], replicated, may hold values from -10 to 4
- skip_gain: float32 [4096], replicated, may hold values from 0.5 to 1.5
Outputs:
- attn_out: bfloat16 [48, 2048, 4096], P('chan', 'seq')
- ssm_out: bfloat16 [48, 2048, 4096], P('chan', None, 'seq')
The draws below stay inside these ranges and needn't reach their ends.
Inputs may be any that keep to these rules, and one draw needn't show every extreme that they name: `doc_lengths`: each row's entries are the lengths of its 16 documents in order and sum to 2048; some document of every row is 256 long.
All inputs are finite; a program needn't handle non-finite values.
Results may differ from the reference program's by a relative error of at most 0.0091.
Values may be sent and summed in bfloat16 or wider, within the bound.
A program may use at most 128 MiB of HBM per device.

```python
import math
import jax
import jax.numpy as jnp
import numpy as np
from jax import lax

QUERY_HEADS = 32
KEY_VALUE_HEADS = 8
HEAD_SIZE = 128
NS = 16
RANK = 256
CH = 4096
TOK_DEV = 128
REACH = 2
NDOCS = 16
ROW_POSITIONS = 2048
STREAM_ROWS = 48
STREAM = 98304
DOCMAX = 256
N_SEQ = 16


def paired_heads(key):
    base_key = jax.random.fold_in(key, 11)
    key_sample, query_draw = jax.random.split(base_key, 2)
    rows_of_keys = jax.random.truncated_normal(key_sample, -6.0, 6.0, (STREAM_ROWS, ROW_POSITIONS, KEY_VALUE_HEADS * HEAD_SIZE), jnp.float32)
    rows_of_queries = jax.random.truncated_normal(query_draw, -6.0, 6.0, (STREAM_ROWS, ROW_POSITIONS, QUERY_HEADS * HEAD_SIZE), jnp.float32)
    return (rows_of_queries, rows_of_keys)


def draw_queries(key, part):
    return paired_heads(key)[0].astype(jnp.bfloat16)


def draw_keys(key, part):
    return paired_heads(key)[1].astype(jnp.bfloat16)


def draw_a_log(key, part):
    flip_draw, slow_draw, fast_draw = jax.random.split(jax.random.fold_in(key, 23), 3)
    slow_share = 0.5
    slow_mask = jax.random.bernoulli(flip_draw, slow_share, (CH, NS))
    chain_log = math.log(0.0015 * STREAM)
    slow_values = jax.random.uniform(slow_draw, (CH, NS), jnp.float32, math.log(0.1), 0.0) - chain_log
    fast_values = jax.random.uniform(fast_draw, (CH, NS), jnp.float32, -chain_log, -math.log(0.0015 * 30.0))
    return jnp.where(slow_mask, slow_values, fast_values)


def steps_of(own_key, extent, shards, smallest, largest):
    def one(axis_at, parts):
        draws = jax.random.uniform(jax.random.fold_in(jax.random.fold_in(own_key, 6), axis_at), (parts,), jnp.float32, smallest / len(shards), largest / len(shards))
        return jnp.repeat(jnp.exp(draws), extent[axis_at] // parts).reshape((-1,) + (1,) * (len(extent) - axis_at - 1))

    loudness = one(*shards[0])
    for cut in shards[1:]:
        loudness = loudness * one(*cut)
    return loudness


def split_up(count, total, limit, skew):
    loads = [(1 << 20) // math.isqrt(standing ** skew) + 1 for standing in range(2, count + 1)]
    spare, holding = total - limit - (count - 1), [1] * (count - 1)
    while spare > 0:
        free = [i for i in range(count - 1) if holding[i] < limit]
        mass, remaining = sum([loads[i] for i in free]), spare
        for i in free:
            addition = min(limit - holding[i], max(1, remaining * loads[i] // mass), spare)
            holding[i] = holding[i] + addition
            spare = spare - addition
    return np.array([limit] + holding)


def ragged_sizes(rng, count, total, bound, lean):
    if count == 2:
        one = jax.random.randint(rng, (), max(1, total - bound), min(bound, total - 1) + 1)
        return jnp.stack([one, total - one])
    tallies = jnp.asarray(split_up(count, total, bound, lean), jnp.int32)
    couples = (count - 1) // 2
    giver, receiver = tallies[1:1 + 2 * couples:2], tallies[2:2 + 2 * couples:2]
    slack = jnp.minimum(giver - 1, bound - receiver)
    shifted = jax.random.randint(jax.random.fold_in(rng, 1), (couples,), 0, 1 << 20) % (slack + 1)
    tallies = tallies.at[1:1 + 2 * couples:2].set(giver - shifted).at[2:2 + 2 * couples:2].set(receiver + shifted)
    return tallies[jax.random.permutation(jax.random.fold_in(rng, 2), count)]


def centred(own_key, dims, scale, reach, shards=(), kind=jnp.bfloat16):
    array = jax.random.normal(own_key, dims, jnp.float32) * scale
    if len(shards) > 0:
        array = steps_of(own_key, dims, shards, -0.22, 0.18) * array
    return jnp.clip(array, min=-reach, max=reach).astype(kind)


def setup_inputs(seed: int = 0) -> dict:
    seeds = jax.random.split(jax.random.key(seed), 11)
    queries = draw_queries(jax.random.fold_in(seeds[10], 71), 0)
    keys = draw_keys(jax.random.fold_in(seeds[10], 71), 0)
    values = centred(seeds[2], (STREAM_ROWS, ROW_POSITIONS, KEY_VALUE_HEADS * HEAD_SIZE), 1.0, 6.0, ((0, 48), (1, 16)))
    doc_lengths = jax.vmap(lambda own: ragged_sizes(own, NDOCS, ROW_POSITIONS, DOCMAX, 2))(jax.random.split(seeds[3], STREAM_ROWS)).reshape((STREAM_ROWS, NDOCS)).astype(jnp.int32)
    rank_in = centred(seeds[4], (CH, RANK), CH ** -0.5, 0.09375)
    bc_weight = centred(seeds[5], (CH, 2 * NS), CH ** -0.5, 0.09375)
    rank_out = centred(seeds[6], (RANK, CH), RANK ** -0.5, 0.375)
    dt_bias = jnp.clip(jax.random.uniform(seeds[7], (CH,), jnp.float32, -8.0, -6.0), -8.0, -6.0)
    a_log = draw_a_log(jax.random.fold_in(seeds[10], 71), 0)
    skip_gain = jnp.clip(jax.random.uniform(seeds[9], (CH,), jnp.float32, 0.5, 1.5), 0.5, 1.5)
    return {"queries": queries, "keys": keys, "values": values, "doc_lengths": doc_lengths, "rank_in": rank_in, "bc_weight": bc_weight, "rank_out": rank_out, "dt_bias": dt_bias, "a_log": a_log, "skip_gain": skip_gain}


masked_fill = -1e+30

def doc_numbers(positions, doc_bounds):
    return lax.optimization_barrier(jnp.sum((doc_bounds[None, :] <= positions[:, None]).astype(jnp.int32), axis=1))

def attend_core(query_tile, key_tile, value_tile, query_pos, key_pos, doc_bounds):
    query_row_count = query_tile.shape[0]
    key_row_count = key_tile.shape[0]
    positions_per_row = QUERY_HEADS // KEY_VALUE_HEADS
    heads_for_queries = query_tile.astype(jnp.float32).reshape(query_row_count, KEY_VALUE_HEADS, positions_per_row, HEAD_SIZE)
    heads_for_keys = key_tile.astype(jnp.float32).reshape(key_row_count, KEY_VALUE_HEADS, HEAD_SIZE)
    heads_for_values = value_tile.astype(jnp.float32).reshape(key_row_count, KEY_VALUE_HEADS, HEAD_SIZE)
    scores = jnp.einsum('tgjd,kgd->gjtk', heads_for_queries, heads_for_keys) * (1.0 / math.sqrt(HEAD_SIZE))
    allowed = (key_pos[None, :] <= query_pos[:, None]) & (key_pos[None, :] >= 0)
    allowed = allowed & (doc_numbers(key_pos, doc_bounds)[None, :] == doc_numbers(query_pos, doc_bounds)[:, None])
    scores = jnp.where(allowed[None, None], scores, masked_fill)
    peak = lax.optimization_barrier(jnp.max(scores, axis=3, keepdims=True))
    raw_weights = jnp.exp(scores - peak)
    weights = (raw_weights / lax.optimization_barrier(jnp.sum(raw_weights, axis=3, keepdims=True))).astype(jnp.bfloat16)
    mixed = jnp.einsum('gjtk,kgd->tgjd', weights.astype(jnp.float32), heads_for_values)
    return mixed.reshape(query_row_count, QUERY_HEADS * HEAD_SIZE).astype(jnp.bfloat16)

def reference(queries, keys, values, doc_lengths, rank_in, bc_weight, rank_out, dt_bias, a_log, skip_gain):
    padding_rows = REACH * TOK_DEV
    window_rows = padding_rows + TOK_DEV

    def attend_row(row_data):
        query_row, single_key_row, single_value_row, row_lengths = row_data
        doc_bounds = jnp.cumsum(row_lengths).astype(jnp.int32)
        padded_keys = jnp.concatenate([jnp.zeros((padding_rows, KEY_VALUE_HEADS * HEAD_SIZE), single_key_row.dtype), single_key_row], axis=0)
        padded_values = jnp.concatenate([jnp.zeros((padding_rows, KEY_VALUE_HEADS * HEAD_SIZE), single_value_row.dtype), single_value_row], axis=0)

        def attend_block(block_index):
            first_row = (block_index * TOK_DEV).astype(jnp.int32)
            query_tile = lax.dynamic_slice_in_dim(query_row, first_row, TOK_DEV, 0)
            key_tile = lax.dynamic_slice_in_dim(padded_keys, first_row, window_rows, 0)
            value_tile = lax.dynamic_slice_in_dim(padded_values, first_row, window_rows, 0)
            query_pos = first_row + jnp.arange(TOK_DEV, dtype=jnp.int32)
            key_pos = first_row - padding_rows + jnp.arange(window_rows, dtype=jnp.int32)
            return attend_core(query_tile, key_tile, value_tile, query_pos, key_pos, doc_bounds)
        block_outs = lax.map(attend_block, jnp.arange(N_SEQ, dtype=jnp.int32))
        return block_outs.reshape(ROW_POSITIONS, QUERY_HEADS * HEAD_SIZE)
    attn_out = lax.map(attend_row, (queries, keys, values, doc_lengths))
    stream = attn_out.reshape(STREAM, CH)
    dt_low = jnp.dot(stream, rank_in, preferred_element_type=jnp.float32).astype(jnp.bfloat16)
    state_maps = jnp.dot(stream, bc_weight, preferred_element_type=jnp.float32)
    decay_rates = -jnp.exp(a_log)

    def outer_step(carry_state, block_data):
        low_block, maps_block, input_block = block_data
        step_sizes = jax.nn.softplus(jnp.dot(low_block, rank_out, preferred_element_type=jnp.float32) + dt_bias)
        input_float = input_block.astype(jnp.float32)

        def inner_step(inner_state, item_data):
            step_row, input_row, maps_row = item_data
            next_state = jnp.exp(step_row[:, None] * decay_rates) * inner_state
            next_state = next_state + (step_row * input_row)[:, None] * maps_row[None, :NS]
            return (next_state, lax.optimization_barrier(jnp.sum(next_state * maps_row[None, NS:], axis=1)))
        carry_state, outputs = lax.scan(inner_step, carry_state, (step_sizes, input_float, maps_block))
        return (carry_state, outputs + skip_gain[None, :] * input_float)
    block_count = STREAM // TOK_DEV
    start_state = jnp.zeros((CH, NS), jnp.float32)
    _, outputs = lax.scan(outer_step, start_state, (dt_low.reshape(block_count, TOK_DEV, RANK), state_maps.reshape(block_count, TOK_DEV, 2 * NS), stream.reshape(block_count, TOK_DEV, CH)))
    ssm_out = outputs.reshape(STREAM_ROWS, ROW_POSITIONS, CH).astype(jnp.bfloat16)
    return (attn_out, ssm_out)
```

```python
import functools
import math

import jax
import jax.numpy as jnp
from jax import lax
from jax.experimental import pallas as pl
from jax.experimental.pallas import tpu as pltpu
from jax.sharding import PartitionSpec as P

NS = 16
TOK = 128
SEGS = 16
PAR = 2
CW = 256
PACK = 160
ORDER = (1, 7, 2, 6, 0, 3, 5, 4)
LOG2E = 1.4426950408889634
MESH = pl.DeviceIdType.MESH
F32 = jnp.float32
BF16 = jnp.bfloat16
VMEM_LIMIT = 60 * 1024 * 1024


def dot(a, b, ca=1, cb=0):
    return lax.dot_general(a, b, (((ca,), (cb,)), ((), ())), preferred_element_type=F32)


def softplus(v):
    z = jnp.exp(-jnp.abs(v))
    series = z * (1.0 - z * (0.5 - z * (1.0 / 3.0 - z * 0.25)))
    return jnp.maximum(v, 0.0) + jnp.where(z < 0.03125, series, jnp.log(1.0 + z))


def attend_kernel(
    doc, q_hbm, k_hbm, v_hbm, rin_hbm, bcw_hbm,
    attn_hbm, xr_hbm, pk,
    qb, kb, vb, wb, bb, ab, po,
    loc_sem, kv_send, kv_recv, x_send, x_recv, p_send, p_recv,
):
    s = lax.axis_index("seq")
    y = lax.div(s, 2)
    c = lax.rem(s, 2)
    sib = s + 1 - 2 * c

    def local(src, dst, i):
        return pltpu.make_async_copy(src, dst, loc_sem.at[i])

    def remote(src, dst, send, recv, to):
        return pltpu.make_async_remote_copy(
            src_ref=src, dst_ref=dst, send_sem=send, recv_sem=recv,
            device_id={"seq": to}, device_id_type=MESH,
        )

    loads = [
        local(k_hbm.at[0], kb.at[0], 0),
        local(q_hbm.at[0], qb, 1),
        local(v_hbm.at[0], vb.at[0], 2),
        local(rin_hbm, wb, 3),
        local(bcw_hbm, bb, 4),
    ]
    barrier = pltpu.get_barrier_semaphore()
    for d in range(1, 16):
        pl.semaphore_signal(
            barrier, inc=1, device_id={"seq": lax.rem(s + d, 16)}, device_id_type=MESH
        )
    for one in loads:
        one.start()

    @pl.when(s < 1)
    def _():
        kb[1] = jnp.zeros_like(kb[1])
        vb[1] = jnp.zeros_like(vb[1])

    @pl.when(s < 2)
    def _():
        kb[2] = jnp.zeros_like(kb[2])
        vb[2] = jnp.zeros_like(vb[2])

    first = s * TOK
    qpos = first + lax.broadcasted_iota(jnp.int32, (TOK, TOK), 0)
    lane = lax.broadcasted_iota(jnp.int32, (TOK, TOK), 1)
    begin = jnp.zeros((TOK, TOK), jnp.int32)
    bound = jnp.int32(0)
    for j in range(16):
        bound = bound + doc[0, j]
        begin = jnp.where(qpos >= bound, bound, begin)
    masks = []
    for b in range(3):
        kpos = first - b * TOK + lane
        masks.append((kpos <= qpos) & (kpos >= begin))

    pl.semaphore_wait(barrier, 15)

    k_own, v_own = k_hbm.at[0], v_hbm.at[0]
    to1 = lax.rem(s + 1, 16)
    to2 = lax.rem(s + 2, 16)
    send1 = [remote(o, d.at[1], kv_send.at[0, i], kv_recv.at[0, i], to1)
             for i, (o, d) in enumerate(((k_own, kb), (v_own, vb)))]
    send2 = [remote(o, d.at[2], kv_send.at[1, i], kv_recv.at[1, i], to2)
             for i, (o, d) in enumerate(((k_own, kb), (v_own, vb)))]
    pass2 = [remote(d.at[1], d.at[2], kv_send.at[2, i], kv_recv.at[1, i], sib)
             for i, d in enumerate((kb, vb))]
    for i in range(2):
        @pl.when(s < 15)
        def _():
            send1[i].start()

        @pl.when((c == 0) & (s < 14))
        def _():
            send2[i].start()

    for i in range(2):
        @pl.when(s >= 1)
        def _():
            send1[i].wait_recv()

        @pl.when((c == 0) & (s >= 2))
        def _():
            pass2[i].start()

    for one in loads[:3]:
        one.wait()
    for i in range(2):
        @pl.when(s >= 2)
        def _():
            send2[i].wait_recv()

    def send_tiles(g):
        for cc in range(2):
            to = 2 * g + cc
            cols = pl.ds(pl.multiple_of(to * CW, CW), CW)
            here = pl.ds(pl.multiple_of(s * TOK, TOK), TOK)

            @pl.when(to != s)
            def _():
                remote(ab.at[:, cols], xr_hbm.at[here], x_send.at[to], x_recv.at[s], to).start()

            @pl.when(to == s)
            def _():
                local(ab.at[:, cols], xr_hbm.at[here], 5).start()

    def group(i):
        off = jnp.int32(0)
        for at, value in enumerate(ORDER):
            off = jnp.where(i == at, value, off)
        return lax.rem(y + off, 8)

    scale = LOG2E / math.sqrt(128.0)

    def step(i, _):
        g = group(i)
        qcols = pl.ds(pl.multiple_of(g * 512, 512), 512)
        kcols = pl.ds(pl.multiple_of(g * 128, 128), 128)
        keys = [kb[b, :, kcols] for b in range(3)]
        vals = [vb[b, :, kcols] for b in range(3)]
        for j in range(4):
            hcols = pl.ds(pl.multiple_of(g * 512 + j * 128, 128), 128)
            q = qb[:, hcols]
            t = [jnp.where(masks[b], dot(q, keys[b], 1, 1) * scale, -1e30) for b in range(3)]
            top = jnp.max(jnp.maximum(jnp.maximum(t[0], t[1]), t[2]), axis=1, keepdims=True)
            e = [jnp.exp2(one - top) for one in t]
            inv = 1.0 / jnp.sum(e[0] + e[1] + e[2], axis=1, keepdims=True)
            o = dot((e[0] * inv).astype(BF16), vals[0])
            o = o + dot((e[1] * inv).astype(BF16), vals[1])
            o = o + dot((e[2] * inv).astype(BF16), vals[2])
            ab[:, hcols] = o.astype(BF16)

        @pl.when((i > 0) & (i < 6))
        def _():
            send_tiles(group(i - 1))

        return 0

    lax.fori_loop(0, 8, step, 0)
    out_copy = local(ab, attn_hbm.at[0], 6)
    out_copy.start()

    loads[3].wait()
    loads[4].wait()
    x = ab[...]
    po[pl.ds(0, TOK), :] = dot(x, wb[...]).astype(BF16)
    bct = dot(bb[...], x, 1, 1)
    po[pl.ds(TOK, 2 * NS), :] = jnp.concatenate([bct, bct], axis=1).astype(BF16)

    own = local(po, pk.at[s], 7)
    own.start()

    def slot(chip, core):
        return 2 * lax.rem(chip + 8, 8) + core

    right = slot(y + 1, c)
    left = slot(y - 1, c)
    ring = {}
    across = {}
    across[0] = remote(po, pk.at[s], p_send.at[7], p_recv.at[s], sib)
    ring[("r", 0)] = remote(po, pk.at[s], p_send.at[0], p_recv.at[s], right)
    ring[("l", 0)] = remote(po, pk.at[s], p_send.at[4], p_recv.at[s], left)
    ring[("r", 0)].start()
    ring[("l", 0)].start()
    across[0].start()
    send_tiles(group(5))

    def arrived(at):
        remote(po, pk.at[at], p_send.at[0], p_recv.at[at], sib).wait_recv()

    for k in range(1, 5):
        at = slot(y - k, c)
        arrived(at)
        if k < 4:
            ring[("r", k)] = remote(pk.at[at], pk.at[at], p_send.at[k], p_recv.at[at], right)
            ring[("r", k)].start()
        across[k] = remote(pk.at[at], pk.at[at], p_send.at[7 + k], p_recv.at[at], sib)
        across[k].start()
        if k < 4:
            at = slot(y + k, c)
            arrived(at)
            if k < 3:
                ring[("l", k)] = remote(pk.at[at], pk.at[at], p_send.at[4 + k], p_recv.at[at], left)
                ring[("l", k)].start()
            across[-k] = remote(pk.at[at], pk.at[at], p_send.at[11 + k], p_recv.at[at], sib)
            across[-k].start()
        if k < 3:
            send_tiles(group(5 + k))

    for k in range(-3, 5):
        arrived(slot(y + k, 1 - c))
    own.wait()
    out_copy.wait()
    for one in list(ring.values()) + list(across.values()):
        one.wait_send()
    for i in range(2):
        @pl.when(s < 15)
        def _():
            send1[i].wait_send()

        @pl.when((c == 0) & (s < 14))
        def _():
            send2[i].wait_send()

        @pl.when((c == 0) & (s >= 2))
        def _():
            pass2[i].wait_send()
    local(ab.at[:, pl.ds(0, CW)], xr_hbm.at[pl.ds(0, TOK)], 5).wait()
    for d in range(1, 16):
        frm = lax.rem(s + d, 16)
        one = remote(
            ab.at[:, pl.ds(0, CW)], xr_hbm.at[pl.ds(0, TOK)], x_send.at[frm], x_recv.at[frm], frm
        )
        one.wait_send()
        one.wait_recv()


def attend(doc, queries, keys, values, rank_in, bc_weight):
    anyspace = pl.BlockSpec(memory_space=pl.ANY)
    return pl.pallas_call(
        attend_kernel,
        out_shape=(
            jax.ShapeDtypeStruct((1, TOK, 4096), BF16),
            jax.ShapeDtypeStruct((SEGS * TOK, CW), BF16),
            jax.ShapeDtypeStruct((SEGS, PACK, CW), BF16),
        ),
        in_specs=[pl.BlockSpec(memory_space=pltpu.SMEM)] + [anyspace] * 5,
        out_specs=(anyspace, anyspace, pl.BlockSpec(memory_space=pltpu.VMEM)),
        scratch_shapes=[
            pltpu.VMEM((TOK, 4096), BF16),
            pltpu.VMEM((3, TOK, 1024), BF16),
            pltpu.VMEM((3, TOK, 1024), BF16),
            pltpu.VMEM((4096, 256), BF16),
            pltpu.VMEM((2 * NS, 4096), BF16),
            pltpu.VMEM((TOK, 4096), BF16),
            pltpu.VMEM((PACK, CW), BF16),
            pltpu.SemaphoreType.DMA((8,)),
            pltpu.SemaphoreType.DMA((3, 2)),
            pltpu.SemaphoreType.DMA((2, 2)),
            pltpu.SemaphoreType.DMA((16,)),
            pltpu.SemaphoreType.DMA((16,)),
            pltpu.SemaphoreType.DMA((15,)),
            pltpu.SemaphoreType.DMA((16,)),
        ],
        compiler_params=pltpu.CompilerParams(
            collective_id=0, has_side_effects=True, vmem_limit_bytes=VMEM_LIMIT
        ),
        name="attend",
    )(doc, queries, keys, values, rank_in, bc_weight)


def scan_kernel(
    x, pk, rout_hbm, bias_hbm, alog_hbm, skip_hbm,
    out,
    dt, u, cum, cb, yl, pre, ha, hc, rw, bias, al, skip, bt, tot, pay, grp, xbuf, zbuf,
    loc_sem, xs_sem, xr_sem, zs_sem, zr_sem,
):
    s = lax.axis_index("seq")
    r = lax.axis_index("chan")
    zi = lax.div(r, 4)
    xi = lax.rem(r, 4)
    at = pl.multiple_of(s * CW, CW)
    loads = [
        pltpu.make_async_copy(rout_hbm.at[:, pl.ds(at, CW)], rw, loc_sem.at[0]),
        pltpu.make_async_copy(bias_hbm.at[:, pl.ds(at, CW)], bias, loc_sem.at[1]),
        pltpu.make_async_copy(alog_hbm.at[:, pl.ds(at, CW)], al, loc_sem.at[2]),
        pltpu.make_async_copy(skip_hbm.at[:, pl.ds(at, CW)], skip, loc_sem.at[3]),
    ]
    for one in loads:
        one.start()
    zbuf[...] = jnp.zeros_like(zbuf)
    xbuf[...] = jnp.zeros_like(xbuf)
    ha[...] = jnp.zeros_like(ha)
    hc[...] = jnp.zeros_like(hc)

    barrier = pltpu.get_barrier_semaphore()

    def chan(zz, xx):
        return 4 * lax.rem(zz + 12, 12) + lax.rem(xx + 4, 4)

    for d in range(1, 4):
        pl.semaphore_signal(barrier, inc=1, device_id={"chan": chan(zi, xi + d)}, device_id_type=MESH)
    for d in range(1, 12):
        pl.semaphore_signal(barrier, inc=1, device_id={"chan": chan(zi + d, xi)}, device_id_type=MESH)
    for one in loads:
        one.wait()

    rate = -jnp.exp(al[...]) * LOG2E
    rates = (rate[:8], rate[8:])

    row = lax.broadcasted_iota(jnp.int32, (TOK, TOK), 0)
    col = lax.broadcasted_iota(jnp.int32, (TOK, TOK), 1)
    tri = (col <= row).astype(BF16)
    spread = (lax.rem(lax.broadcasted_iota(jnp.int32, (NS, CW), 1), NS)
              == lax.broadcasted_iota(jnp.int32, (NS, CW), 0)).astype(BF16)
    block = (lax.div(lax.broadcasted_iota(jnp.int32, (TOK, CW), 1), NS)
             == lax.rem(lax.broadcasted_iota(jnp.int32, (TOK, CW), 0), NS))

    def prepare(q, _):
        for j in range(4):
            seg = q * 4 + j
            rows = pl.ds(pl.multiple_of(seg * TOK, TOK), TOK)
            low = pk[seg, pl.ds(0, TOK), :]
            step = softplus(dot(low, rw[...]) + bias[...])
            dt[rows, :] = step
            u[rows, :] = step * x[rows, :].astype(F32)
            hi = step.astype(BF16)
            lo = (step - hi.astype(F32)).astype(BF16)
            run = dot(tri, hi) + dot(tri, lo)
            cum[rows, :] = run
            tot[pl.ds(seg, 1), :] = run[TOK - 1:, :]
            maps = pk[seg, pl.ds(TOK, 2 * NS), pl.ds(0, TOK)]
            bt[pl.ds(pl.multiple_of(seg * NS, NS), NS), :] = maps[:NS].astype(F32)
            wide_c = dot(maps[NS:], spread, 0, 0)
            cb[rows, :] = jnp.where(block, wide_c, 0.0).astype(BF16)
        return 0

    lax.fori_loop(0, SEGS // 4, prepare, 0)

    def rows_of(seg, chunk):
        return pl.ds(pl.multiple_of(seg * TOK + chunk * 16, 16), 16)

    def pair(p, _):
        def body(q, carry):
            states, maps = carry
            states = [list(one) for one in states]
            for half, (held, ready) in enumerate(((ha, hc), (hc, ha))):
                for k in range(PAR):
                    if half == 0:
                        wrapped = q == 0
                        seg = jnp.where(wrapped, lax.rem(p + 7, 8), p) * PAR + k
                        done = rows_of(seg, jnp.where(wrapped, 7, 2 * q - 1))
                    else:
                        done = rows_of(p * PAR + k, 2 * q)
                    yl[done, :] = dot(cb[done, :], ready[k])
                for t in range(16):
                    for k in range(PAR):
                        at_row = (p * PAR + k) * TOK + (2 * q + half) * 16 + t
                        d = jnp.broadcast_to(dt[pl.ds(at_row, 1), :], (8, CW))
                        w = jnp.broadcast_to(u[pl.ds(at_row, 1), :], (8, CW))
                        lane = half * 16 + t
                        for h in range(2):
                            b = jnp.broadcast_to(maps[k][8 * h: 8 * h + 8, lane: lane + 1], (8, TOK))
                            b = jnp.concatenate([b, b], axis=1)
                            states[k][h] = jnp.exp2(d * rates[h]) * states[k][h] + w * b
                        held[k, pl.ds(16 * t, 16), :] = jnp.concatenate(states[k], axis=0).astype(BF16)
            maps = tuple(pltpu.roll(one, TOK - 32, axis=1) for one in maps)
            return tuple(tuple(one) for one in states), maps

        zero = jnp.zeros((8, CW), F32)
        maps = tuple(
            bt[pl.ds(pl.multiple_of((p * PAR + k) * NS, NS), NS), :] for k in range(PAR)
        )
        states, _ = lax.fori_loop(0, 4, body, (((zero, zero),) * PAR, maps))
        for k in range(PAR):
            pre[p * PAR + k] = jnp.concatenate(states[k], axis=0)
        return 0

    lax.fori_loop(0, SEGS // PAR, pair, 0)
    for k in range(PAR):
        done = rows_of(SEGS - PAR + k, 7)
        yl[done, :] = dot(cb[done, :], hc[k])

    state = jnp.zeros((NS, CW), F32)
    total = jnp.zeros((1, CW), F32)
    for seg in range(SEGS):
        mine = pre[seg]
        t = tot[pl.ds(seg, 1), :]
        pre[seg] = state
        state = jnp.exp2(rate * t) * state + mine
        total = total + t
    pay[pl.ds(0, NS), :] = state
    pay[pl.ds(NS, 8), :] = jnp.broadcast_to(total, (8, CW))
    pl.semaphore_wait(barrier, 14)

    sends = []
    for d in range(1, 4):
        sends.append(pltpu.make_async_remote_copy(
            src_ref=pay, dst_ref=xbuf.at[xi], send_sem=xs_sem.at[d - 1], recv_sem=xr_sem.at[xi],
            device_id={"chan": chan(zi, xi + d)}, device_id_type=MESH))
    for one in sends:
        one.start()
    for d in range(1, 4):
        frm = lax.rem(xi + d, 4)
        pltpu.make_async_remote_copy(
            src_ref=pay, dst_ref=xbuf.at[frm], send_sem=xs_sem.at[d - 1], recv_sem=xr_sem.at[frm],
            device_id={"chan": chan(zi, frm)}, device_id_type=MESH).wait_recv()
    gs = jnp.zeros((NS, CW), F32)
    gt = jnp.zeros((1, CW), F32)
    ms = jnp.zeros((NS, CW), F32)
    mt = jnp.zeros((1, CW), F32)
    own = pay[...]
    for i in range(4):
        got = jnp.where(xi == i, own, xbuf[i])
        os, ot = got[:NS], got[NS: NS + 1]
        dec = jnp.exp2(rate * ot)
        gs = dec * gs + os
        gt = gt + ot
        ms = jnp.where(i < xi, gs, ms)
        mt = jnp.where(i < xi, gt, mt)
    grp[pl.ds(0, NS), :] = gs
    grp[pl.ds(NS, 8), :] = jnp.broadcast_to(gt, (8, CW))

    def zcopy(d, slot):
        return pltpu.make_async_remote_copy(
            src_ref=grp, dst_ref=zbuf.at[slot], send_sem=zs_sem.at[d], recv_sem=zr_sem.at[slot],
            device_id={"chan": chan(zi + d, xi)}, device_id_type=MESH)

    for d in range(11, 0, -1):
        @pl.when(zi + d < 12)
        def _():
            zcopy(d, zi).start()
    for d in range(1, 12):
        @pl.when(zi - d >= 0)
        def _():
            zcopy(d, lax.rem(zi - d + 12, 12)).wait_recv()
    zs = jnp.zeros((NS, CW), F32)
    for i in range(11):
        got = zbuf[i]
        new = jnp.exp2(rate * got[NS: NS + 1]) * zs + got[:NS]
        zs = jnp.where(i < zi, new, zs)
    row_in = jnp.exp2(rate * mt) * zs + ms
    done = jnp.zeros((1, CW), F32)
    for seg in range(SEGS):
        pre[seg] = pre[seg] + jnp.exp2(rate * done) * row_in
        done = done + tot[pl.ds(seg, 1), :]

    def write(rows, ready):
        got = yl[rows, :] + dot(cb[rows, :], ready)
        out[0, rows, :] = (got + skip[...] * x[rows, :].astype(F32)).astype(BF16)

    def carried(q, _):
        seg = lax.div(q, 4)
        start = pre[seg]
        starts = (start[:8], start[8:])
        for half, (held, ready) in enumerate(((ha, hc), (hc, ha))):
            if half == 0:
                before = jnp.where(q == 0, SEGS * TOK - 16, 32 * q - 16)
            else:
                before = 32 * q
            write(pl.ds(pl.multiple_of(before, 16), 16), ready[0])
            for t in range(16):
                d = jnp.broadcast_to(cum[pl.ds(32 * q + 16 * half + t, 1), :], (8, CW))
                g = [jnp.exp2(d * rates[h]) * starts[h] for h in range(2)]
                held[0, pl.ds(16 * t, 16), :] = jnp.concatenate(g, axis=0).astype(BF16)
        return 0

    lax.fori_loop(0, SEGS * TOK // 32, carried, 0)
    write(pl.ds(SEGS * TOK - 16, 16), hc[0])
    for one in sends:
        one.wait_send()
    for d in range(1, 12):
        @pl.when(zi + d < 12)
        def _():
            zcopy(d, zi).wait_send()


def scan(x, pk, rank_out, dt_bias, a_log, skip_gain):
    anyspace = pl.BlockSpec(memory_space=pl.ANY)
    vm = pl.BlockSpec(memory_space=pltpu.VMEM)
    rows = SEGS * TOK
    return pl.pallas_call(
        scan_kernel,
        out_shape=jax.ShapeDtypeStruct((1, rows, CW), BF16),
        in_specs=[vm, vm] + [anyspace] * 4,
        out_specs=vm,
        scratch_shapes=[
            pltpu.VMEM((rows, CW), F32),
            pltpu.VMEM((rows, CW), F32),
            pltpu.VMEM((rows, CW), F32),
            pltpu.VMEM((rows, CW), BF16),
            pltpu.VMEM((rows, CW), F32),
            pltpu.VMEM((SEGS, NS, CW), F32),
            pltpu.VMEM((PAR, 256, CW), BF16),
            pltpu.VMEM((PAR, 256, CW), BF16),
            pltpu.VMEM((256, CW), BF16),
            pltpu.VMEM((1, CW), F32),
            pltpu.VMEM((NS, CW), F32),
            pltpu.VMEM((1, CW), F32),
            pltpu.VMEM((SEGS * NS, TOK), F32),
            pltpu.VMEM((SEGS, CW), F32),
            pltpu.VMEM((24, CW), F32),
            pltpu.VMEM((24, CW), F32),
            pltpu.VMEM((4, 24, CW), F32),
            pltpu.VMEM((12, 24, CW), F32),
            pltpu.SemaphoreType.DMA((4,)),
            pltpu.SemaphoreType.DMA((3,)),
            pltpu.SemaphoreType.DMA((4,)),
            pltpu.SemaphoreType.DMA((12,)),
            pltpu.SemaphoreType.DMA((12,)),
        ],
        compiler_params=pltpu.CompilerParams(
            collective_id=1, has_side_effects=True, vmem_limit_bytes=VMEM_LIMIT
        ),
        name="scan",
    )(x, pk, rank_out, dt_bias, a_log, skip_gain)


def local(
    queries, keys, values, doc_lengths, rank_in, bc_weight, rank_out, dt_bias, a_log, skip_gain
):
    attn_out, x, pk = attend(doc_lengths, queries, keys, values, rank_in, bc_weight.T)
    ssm_out = scan(x, pk, rank_out, dt_bias[None], a_log.T, skip_gain[None])
    return (attn_out, ssm_out)


def solution(mesh):
    return jax.shard_map(
        local,
        mesh=mesh,
        in_specs=(
            P("chan", "seq", None),
            P("chan", "seq", None),
            P("chan", "seq", None),
            P("chan", None),
            P(),
            P(),
            P(),
            P(),
            P(),
            P(),
        ),
        out_specs=(P("chan", "seq", None), P("chan", None, "seq")),
        check_vma=False,
    )
```

```python
import functools
import math

import jax
import jax.numpy as jnp
from jax import lax
from jax.experimental import pallas as pl
from jax.experimental.pallas import tpu as pltpu
from jax.sharding import PartitionSpec as P

NS = 16
TOK = 128
SEGS = 16
PAR = 2
CW = 256
PACK = 160
ORDER = (7, 6, 1, 2, 5, 0, 3, 4)
LOG2E = 1.4426950408889634
MESH = pl.DeviceIdType.MESH
F32 = jnp.float32
BF16 = jnp.bfloat16
VMEM_LIMIT = 60 * 1024 * 1024


def dot(a, b, ca=1, cb=0):
    return lax.dot_general(a, b, (((ca,), (cb,)), ((), ())), preferred_element_type=F32)


def softplus(v):
    z = jnp.exp(-jnp.abs(v))
    series = z * (1.0 - z * (0.5 - z * (1.0 / 3.0 - z * 0.25)))
    return jnp.maximum(v, 0.0) + jnp.where(z < 0.03125, series, jnp.log(1.0 + z))


def attend_kernel(
    doc, q_hbm, k_hbm, v_hbm, rin_hbm, bcw_hbm,
    attn_hbm, xr_hbm, pk,
    qb, kb, vb, wb, bb, ab, po, rb,
    loc_sem, kv_send, kv_recv, x_send, x_recv, p_send, p_recv, r_send, r_recv, f_send,
):
    s = lax.axis_index("seq")
    y = lax.div(s, 2)
    c = lax.rem(s, 2)
    sib = s + 1 - 2 * c

    def local(src, dst, i):
        return pltpu.make_async_copy(src, dst, loc_sem.at[i])

    def remote(src, dst, send, recv, to):
        return pltpu.make_async_remote_copy(
            src_ref=src, dst_ref=dst, send_sem=send, recv_sem=recv,
            device_id={"seq": to}, device_id_type=MESH,
        )

    loads = [
        local(k_hbm.at[0], kb.at[0], 0),
        local(q_hbm.at[0], qb, 1),
        local(v_hbm.at[0], vb.at[0], 2),
        local(rin_hbm, wb, 3),
        local(bcw_hbm, bb, 4),
    ]
    barrier = pltpu.get_barrier_semaphore()
    for d in range(1, 16):
        pl.semaphore_signal(
            barrier, inc=1, device_id={"seq": lax.rem(s + d, 16)}, device_id_type=MESH
        )
    for one in loads:
        one.start()

    @pl.when(s < 1)
    def _():
        kb[1] = jnp.zeros_like(kb[1])
        vb[1] = jnp.zeros_like(vb[1])

    @pl.when(s < 2)
    def _():
        kb[2] = jnp.zeros_like(kb[2])
        vb[2] = jnp.zeros_like(vb[2])

    first = s * TOK
    qpos = first + lax.broadcasted_iota(jnp.int32, (TOK, TOK), 0)
    lane = lax.broadcasted_iota(jnp.int32, (TOK, TOK), 1)
    begin = jnp.zeros((TOK, TOK), jnp.int32)
    bound = jnp.int32(0)
    for j in range(16):
        bound = bound + doc[0, j]
        begin = jnp.where(qpos >= bound, bound, begin)
    masks = []
    for b in range(3):
        kpos = first - b * TOK + lane
        masks.append((kpos <= qpos) & (kpos >= begin))

    pl.semaphore_wait(barrier, 15)

    def group(chip, i):
        off = jnp.int32(0)
        for at, value in enumerate(ORDER):
            off = jnp.where(i == at, value, off)
        return lax.rem(chip + off, 8)

    to1 = lax.rem(s + 1, 16)
    to2 = lax.rem(s + 2, 16)
    both = ((k_hbm.at[0], kb), (v_hbm.at[0], vb))

    def head(chip, i):
        return pl.ds(pl.multiple_of(group(chip, i) * 128, 128), 128)

    def send1(i):
        cols = head(lax.div(to1, 2), i)
        return [remote(o.at[:, cols], d.at[1, :, cols], kv_send.at[0, i, n], kv_recv.at[0, i, n], to1)
                for n, (o, d) in enumerate(both)]

    def send2(i):
        cols = head(lax.div(to2, 2), i)
        return [remote(o.at[:, cols], d.at[2, :, cols], kv_send.at[1, i, n], kv_recv.at[1, i, n], to2)
                for n, (o, d) in enumerate(both)]

    def pass2(i):
        cols = head(y, i)
        return [remote(d.at[1, :, cols], d.at[2, :, cols], kv_send.at[2, i, n], kv_recv.at[1, i, n], sib)
                for n, (o, d) in enumerate(both)]

    def start_kv(i, _):
        for n in range(2):
            @pl.when(s < 15)
            def _():
                send1(i)[n].start()

            @pl.when((c == 0) & (s < 14))
            def _():
                send2(i)[n].start()

        return 0

    lax.fori_loop(0, 8, start_kv, 0)

    def arrive_kv(i):
        cols = head(y, i)
        for n, (o, d) in enumerate(both):
            @pl.when(s >= 1)
            def _():
                remote(d.at[0, :, cols], d.at[1, :, cols], kv_send.at[0, i, n], kv_recv.at[0, i, n], sib).wait_recv()

            @pl.when((c == 0) & (s >= 2))
            def _():
                pass2(i)[n].start()

        for n, (o, d) in enumerate(both):
            @pl.when(s >= 2)
            def _():
                remote(d.at[0, :, cols], d.at[2, :, cols], kv_send.at[1, i, n], kv_recv.at[1, i, n], sib).wait_recv()

    for one in loads[:3]:
        one.wait()

    def send_tiles(g):
        for cc in range(2):
            to = 2 * g + cc
            cols = pl.ds(pl.multiple_of(to * CW, CW), CW)
            here = pl.ds(pl.multiple_of(s * TOK, TOK), TOK)

            @pl.when(to != s)
            def _():
                remote(ab.at[:, cols], xr_hbm.at[here], x_send.at[to], x_recv.at[s], to).start()

            @pl.when(to == s)
            def _():
                local(ab.at[:, cols], xr_hbm.at[here], 5).start()

    scale = LOG2E / math.sqrt(128.0)

    def step(i, _):
        arrive_kv(i)
        g = group(y, i)
        qcols = pl.ds(pl.multiple_of(g * 512, 512), 512)
        kcols = pl.ds(pl.multiple_of(g * 128, 128), 128)
        keys = [kb[b, :, kcols] for b in range(3)]
        vals = [vb[b, :, kcols] for b in range(3)]
        for j in range(4):
            hcols = pl.ds(pl.multiple_of(g * 512 + j * 128, 128), 128)
            q = qb[:, hcols]
            t = [jnp.where(masks[b], dot(q, keys[b], 1, 1) * scale, -1e30) for b in range(3)]
            top = jnp.max(jnp.maximum(jnp.maximum(t[0], t[1]), t[2]), axis=1, keepdims=True)
            e = [jnp.exp2(one - top) for one in t]
            inv = 1.0 / jnp.sum(e[0] + e[1] + e[2], axis=1, keepdims=True)
            o = dot((e[0] * inv).astype(BF16), vals[0])
            o = o + dot((e[1] * inv).astype(BF16), vals[1])
            o = o + dot((e[2] * inv).astype(BF16), vals[2])
            ab[:, hcols] = o.astype(BF16)

        @pl.when((i > 0) & (i < 7))
        def _():
            send_tiles(group(y, i - 1))

        return 0

    lax.fori_loop(0, 8, step, 0)
    out_copy = local(ab, attn_hbm.at[0], 6)
    out_copy.start()

    loads[3].wait()
    loads[4].wait()
    x = ab[...]
    po[pl.ds(0, TOK), :] = dot(x, wb[...]).astype(BF16)
    bct = dot(bb[...], x, 1, 1)
    po[pl.ds(TOK, 2 * NS), :] = jnp.concatenate([bct, bct], axis=1).astype(BF16)

    own = local(po, pk.at[s], 7)
    own.start()

    def slot(chip, core):
        return 2 * lax.rem(chip + 8, 8) + core

    right = slot(y + 1, c)
    left = slot(y - 1, c)
    ring = {}
    across = {}
    across[0] = remote(po, pk.at[s], p_send.at[7], p_recv.at[s], sib)
    ring[("r", 0)] = remote(po, pk.at[s], p_send.at[0], p_recv.at[s], right)
    ring[("l", 0)] = remote(po, pk.at[s], p_send.at[4], p_recv.at[s], left)
    ring[("r", 0)].start()
    ring[("l", 0)].start()
    across[0].start()

    def relay(cc):
        to = 2 * lax.rem(y + 4, 8) + cc
        cols = pl.ds(pl.multiple_of(to * CW, CW), CW)
        return remote(ab.at[:, cols], rb.at[cc], r_send.at[cc], r_recv.at[cc], left)

    def forward(cc):
        frm = slot(y + 1, c)
        here = pl.ds(pl.multiple_of(frm * TOK, TOK), TOK)
        to = 2 * lax.rem(y + 5, 8) + cc
        return remote(rb.at[cc], xr_hbm.at[here], f_send.at[cc], x_recv.at[frm], to)

    for cc in range(2):
        relay(cc).start()

    def arrived(at):
        remote(po, pk.at[at], p_send.at[0], p_recv.at[at], sib).wait_recv()

    for k in range(1, 5):
        at = slot(y - k, c)
        arrived(at)
        if k < 4:
            ring[("r", k)] = remote(pk.at[at], pk.at[at], p_send.at[k], p_recv.at[at], right)
            ring[("r", k)].start()
        across[k] = remote(pk.at[at], pk.at[at], p_send.at[7 + k], p_recv.at[at], sib)
        across[k].start()
        if k < 4:
            at = slot(y + k, c)
            arrived(at)
            if k < 3:
                ring[("l", k)] = remote(pk.at[at], pk.at[at], p_send.at[4 + k], p_recv.at[at], left)
                ring[("l", k)].start()
            across[-k] = remote(pk.at[at], pk.at[at], p_send.at[11 + k], p_recv.at[at], sib)
            across[-k].start()
        if k == 1:
            send_tiles(group(y, 6))
            for cc in range(2):
                relay(cc).wait_recv()
                forward(cc).start()

    for k in range(-3, 5):
        arrived(slot(y + k, 1 - c))
    own.wait()
    out_copy.wait()
    for one in list(ring.values()) + list(across.values()):
        one.wait_send()
    for cc in range(2):
        relay(cc).wait_send()
        forward(cc).wait_send()

    def end_kv(i, _):
        for n in range(2):
            @pl.when(s < 15)
            def _():
                send1(i)[n].wait_send()

            @pl.when((c == 0) & (s < 14))
            def _():
                send2(i)[n].wait_send()

            @pl.when((c == 0) & (s >= 2))
            def _():
                pass2(i)[n].wait_send()

        return 0

    lax.fori_loop(0, 8, end_kv, 0)
    local(ab.at[:, pl.ds(0, CW)], xr_hbm.at[pl.ds(0, TOK)], 5).wait()
    for d in range(1, 16):
        frm = lax.rem(s + d, 16)
        one = remote(
            ab.at[:, pl.ds(0, CW)], xr_hbm.at[pl.ds(0, TOK)], x_send.at[frm], x_recv.at[frm], frm
        )
        one.wait_recv()

        @pl.when(lax.rem(lax.div(frm, 2) + 8 - y, 8) != 4)
        def _():
            one.wait_send()


def attend(doc, queries, keys, values, rank_in, bc_weight):
    anyspace = pl.BlockSpec(memory_space=pl.ANY)
    return pl.pallas_call(
        attend_kernel,
        out_shape=(
            jax.ShapeDtypeStruct((1, TOK, 4096), BF16),
            jax.ShapeDtypeStruct((SEGS * TOK, CW), BF16),
            jax.ShapeDtypeStruct((SEGS, PACK, CW), BF16),
        ),
        in_specs=[pl.BlockSpec(memory_space=pltpu.SMEM)] + [anyspace] * 5,
        out_specs=(anyspace, anyspace, pl.BlockSpec(memory_space=pltpu.VMEM)),
        scratch_shapes=[
            pltpu.VMEM((TOK, 4096), BF16),
            pltpu.VMEM((3, TOK, 1024), BF16),
            pltpu.VMEM((3, TOK, 1024), BF16),
            pltpu.VMEM((4096, 256), BF16),
            pltpu.VMEM((2 * NS, 4096), BF16),
            pltpu.VMEM((TOK, 4096), BF16),
            pltpu.VMEM((PACK, CW), BF16),
            pltpu.VMEM((2, TOK, CW), BF16),
            pltpu.SemaphoreType.DMA((8,)),
            pltpu.SemaphoreType.DMA((3, 8, 2)),
            pltpu.SemaphoreType.DMA((2, 8, 2)),
            pltpu.SemaphoreType.DMA((16,)),
            pltpu.SemaphoreType.DMA((16,)),
            pltpu.SemaphoreType.DMA((15,)),
            pltpu.SemaphoreType.DMA((16,)),
            pltpu.SemaphoreType.DMA((2,)),
            pltpu.SemaphoreType.DMA((2,)),
            pltpu.SemaphoreType.DMA((2,)),
        ],
        compiler_params=pltpu.CompilerParams(
            collective_id=0, has_side_effects=True, vmem_limit_bytes=VMEM_LIMIT
        ),
        name="attend",
    )(doc, queries, keys, values, rank_in, bc_weight)


def scan_kernel(
    x, pk, rout_hbm, bias_hbm, alog_hbm, skip_hbm,
    out,
    dt, u, cum, cb, yl, pre, ha, hc, rw, bias, al, skip, bt, tot, pay, pay_t, grp, grp_t, xbuf, xbuf_t, zbuf, zbuf_t,
    loc_sem, xs_sem, xr_sem, zs_sem, zr_sem,
):
    s = lax.axis_index("seq")
    r = lax.axis_index("chan")
    zi = lax.div(r, 4)
    xi = lax.rem(r, 4)
    at = pl.multiple_of(s * CW, CW)
    loads = [
        pltpu.make_async_copy(rout_hbm.at[:, pl.ds(at, CW)], rw, loc_sem.at[0]),
        pltpu.make_async_copy(bias_hbm.at[:, pl.ds(at, CW)], bias, loc_sem.at[1]),
        pltpu.make_async_copy(alog_hbm.at[:, pl.ds(at, CW)], al, loc_sem.at[2]),
        pltpu.make_async_copy(skip_hbm.at[:, pl.ds(at, CW)], skip, loc_sem.at[3]),
    ]
    for one in loads:
        one.start()
    for one in (zbuf, zbuf_t, xbuf, xbuf_t):
        one[...] = jnp.zeros_like(one)
    ha[...] = jnp.zeros_like(ha)
    hc[...] = jnp.zeros_like(hc)

    barrier = pltpu.get_barrier_semaphore()

    def chan(zz, xx):
        return 4 * lax.rem(zz + 12, 12) + lax.rem(xx + 4, 4)

    for d in range(1, 4):
        pl.semaphore_signal(barrier, inc=1, device_id={"chan": chan(zi, xi + d)}, device_id_type=MESH)
    for d in range(1, 12):
        pl.semaphore_signal(barrier, inc=1, device_id={"chan": chan(zi + d, xi)}, device_id_type=MESH)
    for one in loads:
        one.wait()

    rate = -jnp.exp(al[...]) * LOG2E
    rates = (rate[:8], rate[8:])

    row = lax.broadcasted_iota(jnp.int32, (TOK, TOK), 0)
    col = lax.broadcasted_iota(jnp.int32, (TOK, TOK), 1)
    tri = (col <= row).astype(BF16)
    spread = (lax.rem(lax.broadcasted_iota(jnp.int32, (NS, CW), 1), NS)
              == lax.broadcasted_iota(jnp.int32, (NS, CW), 0)).astype(BF16)
    block = (lax.div(lax.broadcasted_iota(jnp.int32, (TOK, CW), 1), NS)
             == lax.rem(lax.broadcasted_iota(jnp.int32, (TOK, CW), 0), NS))

    def prepare(q, _):
        for j in range(4):
            seg = q * 4 + j
            rows = pl.ds(pl.multiple_of(seg * TOK, TOK), TOK)
            low = pk[seg, pl.ds(0, TOK), :]
            step = softplus(dot(low, rw[...]) + bias[...])
            dt[rows, :] = step
            u[rows, :] = step * x[rows, :].astype(F32)
            hi = step.astype(BF16)
            lo = (step - hi.astype(F32)).astype(BF16)
            run = dot(tri, hi) + dot(tri, lo)
            cum[rows, :] = run
            tot[pl.ds(seg, 1), :] = run[TOK - 1:, :]
            maps = pk[seg, pl.ds(TOK, 2 * NS), pl.ds(0, TOK)]
            bt[pl.ds(pl.multiple_of(seg * NS, NS), NS), :] = maps[:NS].astype(F32)
            wide_c = dot(maps[NS:], spread, 0, 0)
            cb[rows, :] = jnp.where(block, wide_c, 0.0).astype(BF16)
        return 0

    lax.fori_loop(0, SEGS // 4, prepare, 0)

    def rows_of(seg, chunk):
        return pl.ds(pl.multiple_of(seg * TOK + chunk * 16, 16), 16)

    def pair(p, _):
        def body(q, carry):
            states, maps = carry
            states = [list(one) for one in states]
            for half, (held, ready) in enumerate(((ha, hc), (hc, ha))):
                for k in range(PAR):
                    if half == 0:
                        wrapped = q == 0
                        seg = jnp.where(wrapped, lax.rem(p + 7, 8), p) * PAR + k
                        done = rows_of(seg, jnp.where(wrapped, 7, 2 * q - 1))
                    else:
                        done = rows_of(p * PAR + k, 2 * q)
                    yl[done, :] = dot(cb[done, :], ready[k])
                for t in range(16):
                    for k in range(PAR):
                        near = pl.ds(pl.multiple_of((p * PAR + k) * TOK + q * 32, 32), 32)
                        lane = half * 16 + t
                        d = jnp.broadcast_to(dt.at[near][lane: lane + 1, :], (8, CW))
                        w = jnp.broadcast_to(u.at[near][lane: lane + 1, :], (8, CW))
                        for h in range(2):
                            b = jnp.broadcast_to(maps[k][8 * h: 8 * h + 8, lane: lane + 1], (8, TOK))
                            b = jnp.concatenate([b, b], axis=1)
                            states[k][h] = jnp.exp2(d * rates[h]) * states[k][h] + w * b
                        held[k, pl.ds(16 * t, 16), :] = jnp.concatenate(states[k], axis=0).astype(BF16)
            maps = tuple(pltpu.roll(one, TOK - 32, axis=1) for one in maps)
            return tuple(tuple(one) for one in states), maps

        zero = jnp.zeros((8, CW), F32)
        maps = tuple(
            bt[pl.ds(pl.multiple_of((p * PAR + k) * NS, NS), NS), :] for k in range(PAR)
        )
        states, _ = lax.fori_loop(0, 4, body, (((zero, zero),) * PAR, maps))
        for k in range(PAR):
            pre[p * PAR + k] = jnp.concatenate(states[k], axis=0)
        return 0

    lax.fori_loop(0, SEGS // PAR, pair, 0)
    for k in range(PAR):
        done = rows_of(SEGS - PAR + k, 7)
        yl[done, :] = dot(cb[done, :], hc[k])

    state = jnp.zeros((NS, CW), F32)
    total = jnp.zeros((1, CW), F32)
    for seg in range(SEGS):
        mine = pre[seg]
        t = tot[pl.ds(seg, 1), :]
        pre[seg] = state
        state = jnp.exp2(rate * t) * state + mine
        total = total + t
    pay[...] = state.astype(BF16)
    pay_t[...] = total
    pl.semaphore_wait(barrier, 14)

    def xcopy(d, slot):
        to = {"chan": chan(zi, xi + d)}
        return [pltpu.make_async_remote_copy(
            src_ref=o, dst_ref=i.at[slot], send_sem=xs_sem.at[d - 1, n], recv_sem=xr_sem.at[slot, n],
            device_id=to, device_id_type=MESH)
            for n, (o, i) in enumerate(((pay, xbuf), (pay_t, xbuf_t)))]

    for d in range(1, 4):
        for one in xcopy(d, xi):
            one.start()
    for d in range(1, 4):
        for one in xcopy(d, lax.rem(xi + d, 4)):
            one.wait_recv()
    gs = jnp.zeros((NS, CW), F32)
    gt = jnp.zeros((1, CW), F32)
    ms = jnp.zeros((NS, CW), F32)
    mt = jnp.zeros((1, CW), F32)
    for i in range(4):
        os = jnp.where(xi == i, state, xbuf[i].astype(F32))
        ot = jnp.where(xi == i, total, xbuf_t[i])
        dec = jnp.exp2(rate * ot)
        gs = dec * gs + os
        gt = gt + ot
        ms = jnp.where(i < xi, gs, ms)
        mt = jnp.where(i < xi, gt, mt)
    grp[...] = gs.astype(BF16)
    grp_t[...] = gt

    def zcopy(d, slot):
        to = {"chan": chan(zi + d, xi)}
        return [pltpu.make_async_remote_copy(
            src_ref=o, dst_ref=i.at[slot], send_sem=zs_sem.at[d, n], recv_sem=zr_sem.at[slot, n],
            device_id=to, device_id_type=MESH)
            for n, (o, i) in enumerate(((grp, zbuf), (grp_t, zbuf_t)))]

    for d in range(11, 0, -1):
        @pl.when(zi + d < 12)
        def _():
            for one in zcopy(d, zi):
                one.start()
    for d in range(1, 12):
        @pl.when(zi - d >= 0)
        def _():
            for one in zcopy(d, lax.rem(zi - d + 12, 12)):
                one.wait_recv()
    zs = jnp.zeros((NS, CW), F32)
    for i in range(11):
        new = jnp.exp2(rate * zbuf_t[i]) * zs + zbuf[i].astype(F32)
        zs = jnp.where(i < zi, new, zs)
    row_in = jnp.exp2(rate * mt) * zs + ms
    done = jnp.zeros((1, CW), F32)
    for seg in range(SEGS):
        pre[seg] = pre[seg] + jnp.exp2(rate * done) * row_in
        done = done + tot[pl.ds(seg, 1), :]

    def write(rows, ready):
        got = yl[rows, :] + dot(cb[rows, :], ready)
        out[0, rows, :] = (got + skip[...] * x[rows, :].astype(F32)).astype(BF16)

    def carried(q, _):
        seg = lax.div(q, 4)
        start = pre[seg]
        starts = (start[:8], start[8:])
        for half, (held, ready) in enumerate(((ha, hc), (hc, ha))):
            if half == 0:
                before = jnp.where(q == 0, SEGS * TOK - 16, 32 * q - 16)
            else:
                before = 32 * q
            write(pl.ds(pl.multiple_of(before, 16), 16), ready[0])
            for t in range(16):
                near = pl.ds(pl.multiple_of(32 * q, 32), 32)
                d = jnp.broadcast_to(cum.at[near][16 * half + t: 16 * half + t + 1, :], (8, CW))
                g = [jnp.exp2(d * rates[h]) * starts[h] for h in range(2)]
                held[0, pl.ds(16 * t, 16), :] = jnp.concatenate(g, axis=0).astype(BF16)
        return 0

    lax.fori_loop(0, SEGS * TOK // 32, carried, 0)
    write(pl.ds(SEGS * TOK - 16, 16), hc[0])
    for d in range(1, 4):
        for one in xcopy(d, xi):
            one.wait_send()
    for d in range(1, 12):
        @pl.when(zi + d < 12)
        def _():
            for one in zcopy(d, zi):
                one.wait_send()


def scan(x, pk, rank_out, dt_bias, a_log, skip_gain):
    anyspace = pl.BlockSpec(memory_space=pl.ANY)
    vm = pl.BlockSpec(memory_space=pltpu.VMEM)
    rows = SEGS * TOK
    return pl.pallas_call(
        scan_kernel,
        out_shape=jax.ShapeDtypeStruct((1, rows, CW), BF16),
        in_specs=[vm, vm] + [anyspace] * 4,
        out_specs=vm,
        scratch_shapes=[
            pltpu.VMEM((rows, CW), F32),
            pltpu.VMEM((rows, CW), F32),
            pltpu.VMEM((rows, CW), F32),
            pltpu.VMEM((rows, CW), BF16),
            pltpu.VMEM((rows, CW), F32),
            pltpu.VMEM((SEGS, NS, CW), F32),
            pltpu.VMEM((PAR, 256, CW), BF16),
            pltpu.VMEM((PAR, 256, CW), BF16),
            pltpu.VMEM((256, CW), BF16),
            pltpu.VMEM((1, CW), F32),
            pltpu.VMEM((NS, CW), F32),
            pltpu.VMEM((1, CW), F32),
            pltpu.VMEM((SEGS * NS, TOK), F32),
            pltpu.VMEM((SEGS, CW), F32),
            pltpu.VMEM((NS, CW), BF16),
            pltpu.VMEM((1, CW), F32),
            pltpu.VMEM((NS, CW), BF16),
            pltpu.VMEM((1, CW), F32),
            pltpu.VMEM((4, NS, CW), BF16),
            pltpu.VMEM((4, 1, CW), F32),
            pltpu.VMEM((12, NS, CW), BF16),
            pltpu.VMEM((12, 1, CW), F32),
            pltpu.SemaphoreType.DMA((4,)),
            pltpu.SemaphoreType.DMA((3, 2)),
            pltpu.SemaphoreType.DMA((4, 2)),
            pltpu.SemaphoreType.DMA((12, 2)),
            pltpu.SemaphoreType.DMA((12, 2)),
        ],
        compiler_params=pltpu.CompilerParams(
            collective_id=1, has_side_effects=True, vmem_limit_bytes=VMEM_LIMIT
        ),
        name="scan",
    )(x, pk, rank_out, dt_bias, a_log, skip_gain)


def local(
    queries, keys, values, doc_lengths, rank_in, bc_weight, rank_out, dt_bias, a_log, skip_gain
):
    attn_out, x, pk = attend(doc_lengths, queries, keys, values, rank_in, bc_weight.T)
    ssm_out = scan(x, pk, rank_out, dt_bias[None], a_log.T, skip_gain[None])
    return (attn_out, ssm_out)


def solution(mesh):
    return jax.shard_map(
        local,
        mesh=mesh,
        in_specs=(
            P("chan", "seq", None),
            P("chan", "seq", None),
            P("chan", "seq", None),
            P("chan", None),
            P(),
            P(),
            P(),
            P(),
            P(),
            P(),
        ),
        out_specs=(P("chan", "seq", None), P("chan", None, "seq")),
        check_vma=False,
    )
```

```python
import functools
import math

import jax
import jax.numpy as jnp
from jax import lax
from jax.experimental import pallas as pl
from jax.experimental.pallas import tpu as pltpu
from jax.sharding import PartitionSpec as P

NS = 16
TOK = 128
SEGS = 16
PAR = 2
EARLY = 10
CW = 256
PACK = 160
ORDER = (7, 6, 1, 2, 5, 0, 3, 4)
LOG2E = 1.4426950408889634
MESH = pl.DeviceIdType.MESH
F32 = jnp.float32
BF16 = jnp.bfloat16
VMEM_LIMIT = 60 * 1024 * 1024


def dot(a, b, ca=1, cb=0):
    return lax.dot_general(a, b, (((ca,), (cb,)), ((), ())), preferred_element_type=F32)


def softplus(v):
    z = jnp.exp(-jnp.abs(v))
    series = z * (1.0 - z * (0.5 - z * (1.0 / 3.0 - z * 0.25)))
    return jnp.maximum(v, 0.0) + jnp.where(z < 0.03125, series, jnp.log(1.0 + z))


def row_kernel(
    doc, q_hbm, k_hbm, v_hbm, rin_hbm, bcw_hbm, rout_hbm, bias_hbm, alog_hbm, skip_hbm,
    attn_out, out,
    qb, kb, vb, wb, bb, ab, po, rb, x, pk,
    dt, u, cum, cb, yl, ebuf, pre, ha, hc, rw, bias, al, skip, bt, tot,
    pay, pay_t, grp, grp_t, xbuf, xbuf_t, zbuf, zbuf_t,
    loc_sem, kv_send, kv_recv, x_send, x_recv, p_send, p_recv, r_send, r_recv, f_send,
    xs_sem, xr_sem, zs_sem, zr_sem, ready,
):
    s = lax.axis_index("seq")
    y = lax.div(s, 2)
    c = lax.rem(s, 2)
    sib = s + 1 - 2 * c

    at = pl.multiple_of(s * CW, CW)

    def local(src, dst, i):
        return pltpu.make_async_copy(src, dst, loc_sem.at[i])

    def remote(src, dst, send, recv, to):
        return pltpu.make_async_remote_copy(
            src_ref=src, dst_ref=dst, send_sem=send, recv_sem=recv,
            device_id={"seq": to}, device_id_type=MESH,
        )

    loads = [
        local(k_hbm.at[0], kb.at[0], 0),
        local(q_hbm.at[0], qb, 1),
        local(v_hbm.at[0], vb.at[0], 2),
        local(rin_hbm, wb, 3),
        local(bcw_hbm, bb, 4),
        local(rout_hbm.at[:, pl.ds(at, CW)], rw, 8),
        local(bias_hbm.at[:, pl.ds(at, CW)], bias, 9),
        local(alog_hbm.at[:, pl.ds(at, CW)], al, 10),
        local(skip_hbm.at[:, pl.ds(at, CW)], skip, 11),
    ]
    r = lax.axis_index("chan")
    zi = lax.div(r, 4)
    xi = lax.rem(r, 4)

    def chan(zz, xx):
        return 4 * lax.rem(zz + 12, 12) + lax.rem(xx + 4, 4)

    for one in (zbuf, zbuf_t, xbuf, xbuf_t):
        one[...] = jnp.zeros_like(one)
    barrier = pltpu.get_barrier_semaphore()
    for d in range(1, 12):
        @pl.when(zi + d < 12)
        def _():
            pl.semaphore_signal(barrier, inc=1, device_id={"chan": chan(zi + d, xi)}, device_id_type=MESH)
    for d in range(1, 4):
        pl.semaphore_signal(barrier, inc=1, device_id={"chan": chan(zi, xi + d)}, device_id_type=MESH)
    for d in range(1, 16):
        pl.semaphore_signal(
            barrier, inc=1, device_id={"seq": lax.rem(s + d, 16)}, device_id_type=MESH
        )
    for one in loads:
        one.start()

    @pl.when(s < 1)
    def _():
        kb[1] = jnp.zeros_like(kb[1])
        vb[1] = jnp.zeros_like(vb[1])

    @pl.when(s < 2)
    def _():
        kb[2] = jnp.zeros_like(kb[2])
        vb[2] = jnp.zeros_like(vb[2])

    first = s * TOK
    qpos = first + lax.broadcasted_iota(jnp.int32, (TOK, TOK), 0)
    lane = lax.broadcasted_iota(jnp.int32, (TOK, TOK), 1)
    begin = jnp.zeros((TOK, TOK), jnp.int32)
    bound = jnp.int32(0)
    for j in range(16):
        bound = bound + doc[0, j]
        begin = jnp.where(qpos >= bound, bound, begin)
    masks = []
    for b in range(3):
        kpos = first - b * TOK + lane
        masks.append((kpos <= qpos) & (kpos >= begin))

    pl.semaphore_wait(barrier, 18 + zi)
    for d in range(1, 12):
        @pl.when(zi - d >= 0)
        def _():
            pl.semaphore_signal(ready, inc=1, device_id={"chan": chan(zi - d, xi)}, device_id_type=MESH)

    def group(chip, i):
        off = jnp.int32(0)
        for at, value in enumerate(ORDER):
            off = jnp.where(i == at, value, off)
        return lax.rem(chip + off, 8)

    to1 = lax.rem(s + 1, 16)
    to2 = lax.rem(s + 2, 16)
    both = ((k_hbm.at[0], kb), (v_hbm.at[0], vb))

    def head(chip, i):
        return pl.ds(pl.multiple_of(group(chip, i) * 128, 128), 128)

    def send1(i):
        cols = head(lax.div(to1, 2), i)
        return [remote(o.at[:, cols], d.at[1, :, cols], kv_send.at[0, i, n], kv_recv.at[0, i, n], to1)
                for n, (o, d) in enumerate(both)]

    def send2(i):
        cols = head(lax.div(to2, 2), i)
        return [remote(o.at[:, cols], d.at[2, :, cols], kv_send.at[1, i, n], kv_recv.at[1, i, n], to2)
                for n, (o, d) in enumerate(both)]

    def pass2(i):
        cols = head(y, i)
        return [remote(d.at[1, :, cols], d.at[2, :, cols], kv_send.at[2, i, n], kv_recv.at[1, i, n], sib)
                for n, (o, d) in enumerate(both)]

    def start_kv(i, _):
        for n in range(2):
            @pl.when(s < 15)
            def _():
                send1(i)[n].start()

            @pl.when((c == 0) & (s < 14))
            def _():
                send2(i)[n].start()

        return 0

    lax.fori_loop(0, 8, start_kv, 0)

    def arrive_kv(i):
        cols = head(y, i)
        for n, (o, d) in enumerate(both):
            @pl.when(s >= 1)
            def _():
                remote(d.at[0, :, cols], d.at[1, :, cols], kv_send.at[0, i, n], kv_recv.at[0, i, n], sib).wait_recv()

            @pl.when((c == 0) & (s >= 2))
            def _():
                pass2(i)[n].start()

        for n, (o, d) in enumerate(both):
            @pl.when(s >= 2)
            def _():
                remote(d.at[0, :, cols], d.at[2, :, cols], kv_send.at[1, i, n], kv_recv.at[1, i, n], sib).wait_recv()

    for one in loads[:3]:
        one.wait()

    def send_tiles(g):
        for cc in range(2):
            to = 2 * g + cc
            cols = pl.ds(pl.multiple_of(to * CW, CW), CW)
            here = pl.ds(pl.multiple_of(s * TOK, TOK), TOK)

            @pl.when(to != s)
            def _():
                remote(ab.at[:, cols], x.at[here], x_send.at[to], x_recv.at[s], to).start()

            @pl.when(to == s)
            def _():
                local(ab.at[:, cols], x.at[here], 5).start()

    scale = LOG2E / math.sqrt(128.0)

    def step(i, _):
        arrive_kv(i)
        g = group(y, i)
        qcols = pl.ds(pl.multiple_of(g * 512, 512), 512)
        kcols = pl.ds(pl.multiple_of(g * 128, 128), 128)
        keys = [kb[b, :, kcols] for b in range(3)]
        vals = [vb[b, :, kcols] for b in range(3)]
        for j in range(4):
            hcols = pl.ds(pl.multiple_of(g * 512 + j * 128, 128), 128)
            q = qb[:, hcols]
            t = [jnp.where(masks[b], dot(q, keys[b], 1, 1) * scale, -1e30) for b in range(3)]
            top = jnp.max(jnp.maximum(jnp.maximum(t[0], t[1]), t[2]), axis=1, keepdims=True)
            e = [jnp.exp2(one - top) for one in t]
            inv = 1.0 / jnp.sum(e[0] + e[1] + e[2], axis=1, keepdims=True)
            o = dot((e[0] * inv).astype(BF16), vals[0])
            o = o + dot((e[1] * inv).astype(BF16), vals[1])
            o = o + dot((e[2] * inv).astype(BF16), vals[2])
            ab[:, hcols] = o.astype(BF16)

        @pl.when((i > 0) & (i < 7))
        def _():
            send_tiles(group(y, i - 1))

        return 0

    lax.fori_loop(0, 8, step, 0)
    out_copy = local(ab, attn_out.at[0], 6)
    out_copy.start()

    loads[3].wait()
    loads[4].wait()
    toks = ab[...]
    po[pl.ds(0, TOK), :] = dot(toks, wb[...]).astype(BF16)
    bct = dot(bb[...], toks, 1, 1)
    po[pl.ds(TOK, 2 * NS), :] = jnp.concatenate([bct, bct], axis=1).astype(BF16)

    own = local(po, pk.at[s], 7)
    own.start()

    def slot(chip, core):
        return 2 * lax.rem(chip + 8, 8) + core

    right = slot(y + 1, c)
    left = slot(y - 1, c)
    ring = {}
    across = {}
    across[0] = remote(po, pk.at[s], p_send.at[7], p_recv.at[s], sib)
    ring[("r", 0)] = remote(po, pk.at[s], p_send.at[0], p_recv.at[s], right)
    ring[("l", 0)] = remote(po, pk.at[s], p_send.at[4], p_recv.at[s], left)
    ring[("r", 0)].start()
    ring[("l", 0)].start()
    across[0].start()

    def relay(cc):
        to = 2 * lax.rem(y + 4, 8) + cc
        cols = pl.ds(pl.multiple_of(to * CW, CW), CW)
        return remote(ab.at[:, cols], rb.at[cc], r_send.at[cc], r_recv.at[cc], left)

    def forward(cc):
        frm = slot(y + 1, c)
        here = pl.ds(pl.multiple_of(frm * TOK, TOK), TOK)
        to = 2 * lax.rem(y + 5, 8) + cc
        return remote(rb.at[cc], x.at[here], f_send.at[cc], x_recv.at[frm], to)

    for cc in range(2):
        relay(cc).start()

    for one in loads[5:]:
        one.wait()
    rate = -jnp.exp(al[...]) * LOG2E
    rates = (rate[:8], rate[8:])

    row = lax.broadcasted_iota(jnp.int32, (TOK, TOK), 0)
    col = lax.broadcasted_iota(jnp.int32, (TOK, TOK), 1)
    tri = (col <= row).astype(BF16)
    spread = (lax.rem(lax.broadcasted_iota(jnp.int32, (NS, CW), 1), NS)
              == lax.broadcasted_iota(jnp.int32, (NS, CW), 0)).astype(BF16)
    block = (lax.div(lax.broadcasted_iota(jnp.int32, (TOK, CW), 1), NS)
             == lax.rem(lax.broadcasted_iota(jnp.int32, (TOK, CW), 0), NS))

    def prepare(*segs):
        for seg in segs:
            rows = pl.ds(pl.multiple_of(seg * TOK, TOK), TOK)
            low = pk[seg, pl.ds(0, TOK), :]
            step = softplus(dot(low, rw[...]) + bias[...])
            dt[rows, :] = step
            hi = step.astype(BF16)
            lo = (step - hi.astype(F32)).astype(BF16)
            run = dot(tri, hi) + dot(tri, lo)
            cum[rows, :] = run
            tot[pl.ds(seg, 1), :] = run[TOK - 1:, :]
            maps = pk[seg, pl.ds(TOK, 2 * NS), pl.ds(0, TOK)]
            bt[pl.ds(pl.multiple_of(seg * NS, NS), NS), :] = maps[:NS].astype(F32)
            wide_c = dot(maps[NS:], spread, 0, 0)
            cb[rows, :] = jnp.where(block, wide_c, 0.0).astype(BF16)

    def arrived(at):
        remote(po, pk.at[at], p_send.at[0], p_recv.at[at], sib).wait_recv()

    for k in range(1, 5):
        far = slot(y - k, c)
        arrived(far)
        if k < 4:
            ring[("r", k)] = remote(pk.at[far], pk.at[far], p_send.at[k], p_recv.at[far], right)
            ring[("r", k)].start()
        across[k] = remote(pk.at[far], pk.at[far], p_send.at[7 + k], p_recv.at[far], sib)
        across[k].start()
        if k < 4:
            far = slot(y + k, c)
            arrived(far)
            if k < 3:
                ring[("l", k)] = remote(pk.at[far], pk.at[far], p_send.at[4 + k], p_recv.at[far], left)
                ring[("l", k)].start()
            across[-k] = remote(pk.at[far], pk.at[far], p_send.at[11 + k], p_recv.at[far], sib)
            across[-k].start()
        if k == 1:
            send_tiles(group(y, 6))
            for cc in range(2):
                relay(cc).wait_recv()
                forward(cc).start()
            own.wait()
            arrived(slot(y, 1 - c))
            prepare(s, sib)
        elif k < 4:
            for far in (slot(y - k + 1, 1 - c), slot(y + k - 1, 1 - c)):
                arrived(far)
            prepare(slot(y - k + 1, c), slot(y + k - 1, c))
            prepare(slot(y - k + 1, 1 - c), slot(y + k - 1, 1 - c))

    for k in (-3, 3, 4):
        arrived(slot(y + k, 1 - c))
    prepare(slot(y - 3, c), slot(y + 3, c))
    prepare(slot(y - 3, 1 - c), slot(y + 3, 1 - c))
    prepare(slot(y + 4, c), slot(y + 4, 1 - c))

    def tile(of):
        return remote(
            ab.at[:, pl.ds(0, CW)], x.at[pl.ds(0, TOK)], x_send.at[of], x_recv.at[of], of
        )

    local(ab.at[:, pl.ds(0, CW)], x.at[pl.ds(0, TOK)], 5).wait()
    for d in range(1, 16):
        tile(lax.rem(s + d, 16)).wait_recv()

    def drive(seg, _):
        rows = pl.ds(pl.multiple_of(seg * TOK, TOK), TOK)
        u[rows, :] = dt[rows, :] * x[rows, :].astype(F32)
        return 0

    lax.fori_loop(0, SEGS, drive, 0)
    ha[...] = jnp.zeros_like(ha)
    hc[...] = jnp.zeros_like(hc)

    def rows_of(seg, chunk):
        return pl.ds(pl.multiple_of(seg * TOK + chunk * 16, 16), 16)

    def pair(p, _):
        def body(q, carry):
            states, maps = carry
            states = [list(one) for one in states]
            for half, (held, ready) in enumerate(((ha, hc), (hc, ha)) * 2):
                for k in range(PAR):
                    if half == 0:
                        wrapped = q == 0
                        seg = jnp.where(wrapped, lax.rem(p + 7, 8), p) * PAR + k
                        done = rows_of(seg, jnp.where(wrapped, 7, 4 * q - 1))
                    else:
                        done = rows_of(p * PAR + k, 4 * q + half - 1)
                    yl[done, :] = dot(cb[done, :], ready[k])
                for t in range(16):
                    for k in range(PAR):
                        near = pl.ds(pl.multiple_of((p * PAR + k) * TOK + q * 64, 64), 64)
                        lane = half * 16 + t
                        d = jnp.broadcast_to(dt.at[near][lane: lane + 1, :], (8, CW))
                        w = jnp.broadcast_to(u.at[near][lane: lane + 1, :], (8, CW))
                        for h in range(2):
                            b = jnp.broadcast_to(maps[k][8 * h: 8 * h + 8, lane: lane + 1], (8, TOK))
                            b = jnp.concatenate([b, b], axis=1)
                            states[k][h] = jnp.exp2(d * rates[h]) * states[k][h] + w * b
                        held[k, pl.ds(16 * t, 16), :] = jnp.concatenate(states[k], axis=0).astype(BF16)
            maps = tuple(pltpu.roll(one, TOK - 64, axis=1) for one in maps)
            return tuple(tuple(one) for one in states), maps

        zero = jnp.zeros((8, CW), F32)
        maps = tuple(
            bt[pl.ds(pl.multiple_of((p * PAR + k) * NS, NS), NS), :] for k in range(PAR)
        )
        states, _ = lax.fori_loop(0, 2, body, (((zero, zero),) * PAR, maps))
        for k in range(PAR):
            pre[p * PAR + k] = jnp.concatenate(states[k], axis=0)
        return 0

    lax.fori_loop(0, SEGS // PAR, pair, 0)
    for k in range(PAR):
        done = rows_of(SEGS - PAR + k, 7)
        yl[done, :] = dot(cb[done, :], hc[k])

    state = jnp.zeros((NS, CW), F32)
    total = jnp.zeros((1, CW), F32)
    for seg in range(SEGS):
        mine = pre[seg]
        t = tot[pl.ds(seg, 1), :]
        pre[seg] = state
        state = jnp.exp2(rate * t) * state + mine
        total = total + t
    pay[...] = state.astype(BF16)
    pay_t[...] = total

    def xcopy(d, slot):
        to = {"chan": chan(zi, xi + d)}
        return [pltpu.make_async_remote_copy(
            src_ref=o, dst_ref=i.at[slot], send_sem=xs_sem.at[d - 1, n], recv_sem=xr_sem.at[slot, n],
            device_id=to, device_id_type=MESH)
            for n, (o, i) in enumerate(((pay, xbuf), (pay_t, xbuf_t)))]

    for d in range(1, 4):
        for one in xcopy(d, xi):
            one.start()

    def decay(q, _):
        near = pl.ds(pl.multiple_of(64 * q, 64), 64)
        for t in range(64):
            d = jnp.broadcast_to(cum.at[near][t: t + 1, :], (8, CW))
            e = [jnp.exp2(d * rates[h]).astype(BF16) for h in range(2)]
            held = pl.ds(pl.multiple_of(1024 * q + 16 * t, 16), 16)
            ebuf[held, :] = jnp.concatenate(e, axis=0)
        return 0

    lax.fori_loop(0, EARLY, decay, 0)
    for d in range(1, 4):
        for one in xcopy(d, lax.rem(xi + d, 4)):
            one.wait_recv()
    gs = jnp.zeros((NS, CW), F32)
    gt = jnp.zeros((1, CW), F32)
    ms = jnp.zeros((NS, CW), F32)
    mt = jnp.zeros((1, CW), F32)
    for i in range(4):
        os = jnp.where(xi == i, state, xbuf[i].astype(F32))
        ot = jnp.where(xi == i, total, xbuf_t[i])
        dec = jnp.exp2(rate * ot)
        gs = dec * gs + os
        gt = gt + ot
        ms = jnp.where(i < xi, gs, ms)
        mt = jnp.where(i < xi, gt, mt)
    grp[...] = gs.astype(BF16)
    grp_t[...] = gt

    def zcopy(d, slot):
        to = {"chan": chan(zi + d, xi)}
        return [pltpu.make_async_remote_copy(
            src_ref=o, dst_ref=i.at[slot], send_sem=zs_sem.at[d, n], recv_sem=zr_sem.at[slot, n],
            device_id=to, device_id_type=MESH)
            for n, (o, i) in enumerate(((grp, zbuf), (grp_t, zbuf_t)))]


    @pl.when(zi < 11)
    def _():
        pl.semaphore_wait(ready, 11 - zi)

    for d in range(11, 0, -1):
        @pl.when(zi + d < 12)
        def _():
            for one in zcopy(d, zi):
                one.start()
    lax.fori_loop(EARLY, SEGS * TOK // 64, decay, 0)
    for d in range(1, 12):
        @pl.when(zi - d >= 0)
        def _():
            for one in zcopy(d, lax.rem(zi - d + 12, 12)):
                one.wait_recv()
    zs = jnp.zeros((NS, CW), F32)
    for i in range(11):
        new = jnp.exp2(rate * zbuf_t[i]) * zs + zbuf[i].astype(F32)
        zs = jnp.where(i < zi, new, zs)
    row_in = jnp.exp2(rate * mt) * zs + ms
    done = jnp.zeros((1, CW), F32)
    for seg in range(SEGS):
        pre[seg] = pre[seg] + jnp.exp2(rate * done) * row_in
        done = done + tot[pl.ds(seg, 1), :]

    def carried(q, _):
        start = pre[q].astype(BF16)
        starts = jnp.concatenate([start] * 16, axis=0)
        for j in range(8):
            rows = pl.ds(pl.multiple_of(TOK * q + 16 * j, 16), 16)
            held = pl.ds(pl.multiple_of(NS * TOK * q + 256 * j, 256), 256)
            got = yl[rows, :] + dot(cb[rows, :], ebuf[held, :] * starts)
            out[0, rows, :] = (got + skip[...] * x[rows, :].astype(F32)).astype(BF16)
        return 0

    lax.fori_loop(0, SEGS, carried, 0)
    out_copy.wait()
    for one in list(ring.values()) + list(across.values()):
        one.wait_send()
    for cc in range(2):
        relay(cc).wait_send()
        forward(cc).wait_send()

    def end_kv(i, _):
        for n in range(2):
            @pl.when(s < 15)
            def _():
                send1(i)[n].wait_send()

            @pl.when((c == 0) & (s < 14))
            def _():
                send2(i)[n].wait_send()

            @pl.when((c == 0) & (s >= 2))
            def _():
                pass2(i)[n].wait_send()

        return 0

    lax.fori_loop(0, 8, end_kv, 0)
    for d in range(1, 16):
        to = lax.rem(s + d, 16)

        @pl.when(lax.rem(lax.div(to, 2) + 8 - y, 8) != 4)
        def _():
            tile(to).wait_send()

    for d in range(1, 4):
        for one in xcopy(d, xi):
            one.wait_send()
    for d in range(1, 12):
        @pl.when(zi + d < 12)
        def _():
            for one in zcopy(d, zi):
                one.wait_send()


def row(doc, queries, keys, values, rank_in, bc_weight, rank_out, dt_bias, a_log, skip_gain):
    anyspace = pl.BlockSpec(memory_space=pl.ANY)
    rows = SEGS * TOK
    return pl.pallas_call(
        row_kernel,
        out_shape=(
            jax.ShapeDtypeStruct((1, TOK, 4096), BF16),
            jax.ShapeDtypeStruct((1, rows, CW), BF16),
        ),
        in_specs=[pl.BlockSpec(memory_space=pltpu.SMEM)] + [anyspace] * 9,
        out_specs=(anyspace, pl.BlockSpec(memory_space=pltpu.VMEM)),
        scratch_shapes=[
            pltpu.VMEM((TOK, 4096), BF16),
            pltpu.VMEM((3, TOK, 1024), BF16),
            pltpu.VMEM((3, TOK, 1024), BF16),
            pltpu.VMEM((4096, 256), BF16),
            pltpu.VMEM((2 * NS, 4096), BF16),
            pltpu.VMEM((TOK, 4096), BF16),
            pltpu.VMEM((PACK, CW), BF16),
            pltpu.VMEM((2, TOK, CW), BF16),
            pltpu.VMEM((rows, CW), BF16),
            pltpu.VMEM((SEGS, PACK, CW), BF16),
            pltpu.VMEM((rows, CW), F32),
            pltpu.VMEM((rows, CW), F32),
            pltpu.VMEM((rows, CW), F32),
            pltpu.VMEM((rows, CW), BF16),
            pltpu.VMEM((rows, CW), F32),
            pltpu.VMEM((rows * NS, CW), BF16),
            pltpu.VMEM((SEGS, NS, CW), F32),
            pltpu.VMEM((PAR, 256, CW), BF16),
            pltpu.VMEM((PAR, 256, CW), BF16),
            pltpu.VMEM((256, CW), BF16),
            pltpu.VMEM((1, CW), F32),
            pltpu.VMEM((NS, CW), F32),
            pltpu.VMEM((1, CW), F32),
            pltpu.VMEM((SEGS * NS, TOK), F32),
            pltpu.VMEM((SEGS, CW), F32),
            pltpu.VMEM((NS, CW), BF16),
            pltpu.VMEM((1, CW), F32),
            pltpu.VMEM((NS, CW), BF16),
            pltpu.VMEM((1, CW), F32),
            pltpu.VMEM((4, NS, CW), BF16),
            pltpu.VMEM((4, 1, CW), F32),
            pltpu.VMEM((12, NS, CW), BF16),
            pltpu.VMEM((12, 1, CW), F32),
            pltpu.SemaphoreType.DMA((12,)),
            pltpu.SemaphoreType.DMA((3, 8, 2)),
            pltpu.SemaphoreType.DMA((2, 8, 2)),
            pltpu.SemaphoreType.DMA((16,)),
            pltpu.SemaphoreType.DMA((16,)),
            pltpu.SemaphoreType.DMA((15,)),
            pltpu.SemaphoreType.DMA((16,)),
            pltpu.SemaphoreType.DMA((2,)),
            pltpu.SemaphoreType.DMA((2,)),
            pltpu.SemaphoreType.DMA((2,)),
            pltpu.SemaphoreType.DMA((3, 2)),
            pltpu.SemaphoreType.DMA((4, 2)),
            pltpu.SemaphoreType.DMA((12, 2)),
            pltpu.SemaphoreType.DMA((12, 2)),
            pltpu.SemaphoreType.REGULAR,
        ],
        compiler_params=pltpu.CompilerParams(
            collective_id=0, has_side_effects=True, vmem_limit_bytes=VMEM_LIMIT
        ),
        name="row",
    )(doc, queries, keys, values, rank_in, bc_weight, rank_out, dt_bias, a_log, skip_gain)


def local(
    queries, keys, values, doc_lengths, rank_in, bc_weight, rank_out, dt_bias, a_log, skip_gain
):
    return row(
        doc_lengths, queries, keys, values, rank_in, bc_weight.T,
        rank_out, dt_bias[None], a_log.T, skip_gain[None],
    )


def solution(mesh):
    return jax.shard_map(
        local,
        mesh=mesh,
        in_specs=(
            P("chan", "seq", None),
            P("chan", "seq", None),
            P("chan", "seq", None),
            P("chan", None),
            P(),
            P(),
            P(),
            P(),
            P(),
            P(),
        ),
        out_specs=(P("chan", "seq", None), P("chan", None, "seq")),
        check_vma=False,
    )
```

```python
import functools
import math

import jax
import jax.numpy as jnp
from jax import lax
from jax.experimental import pallas as pl
from jax.experimental.pallas import tpu as pltpu
from jax.sharding import PartitionSpec as P

NS = 16
TOK = 128
SEGS = 16
PAR = 2
EARLY = 5
CW = 256
PACK = 160
ORDER = (7, 6, 1, 2, 5, 0, 3, 4)
LOG2E = 1.4426950408889634
MESH = pl.DeviceIdType.MESH
F32 = jnp.float32
BF16 = jnp.bfloat16
VMEM_LIMIT = 60 * 1024 * 1024


def dot(a, b, ca=1, cb=0):
    return lax.dot_general(a, b, (((ca,), (cb,)), ((), ())), preferred_element_type=F32)


def softplus(v):
    z = jnp.exp(-jnp.abs(v))
    series = z * (1.0 - z * (0.5 - z * (1.0 / 3.0 - z * 0.25)))
    return jnp.maximum(v, 0.0) + jnp.where(z < 0.03125, series, jnp.log(1.0 + z))


def row_kernel(
    doc, q_hbm, k_hbm, v_hbm, rin_hbm, bcw_hbm, rout_hbm, bias_hbm, alog_hbm, skip_hbm,
    attn_out, out,
    qb, kb, vb, wb, bb, ab, po, rb, x, pk,
    dt, u, cum, cb, yl, ebuf, pre, ha, hc, rw, bias, al, skip, bt, tot,
    pay, pay_t, grp, grp_t, xbuf, xbuf_t, zbuf, zbuf_t,
    loc_sem, kv_send, kv_recv, x_send, x_recv, p_send, p_recv, r_send, r_recv, f_send,
    xs_sem, xr_sem, zs_sem, zr_sem, ready, ready_x,
):
    s = lax.axis_index("seq")
    y = lax.div(s, 2)
    c = lax.rem(s, 2)
    sib = s + 1 - 2 * c

    at = pl.multiple_of(s * CW, CW)

    def local(src, dst, i):
        return pltpu.make_async_copy(src, dst, loc_sem.at[i])

    def remote(src, dst, send, recv, to):
        return pltpu.make_async_remote_copy(
            src_ref=src, dst_ref=dst, send_sem=send, recv_sem=recv,
            device_id={"seq": to}, device_id_type=MESH,
        )

    loads = [
        local(k_hbm.at[0], kb.at[0], 0),
        local(q_hbm.at[0], qb, 1),
        local(v_hbm.at[0], vb.at[0], 2),
        local(rin_hbm, wb, 3),
        local(bcw_hbm, bb, 4),
        local(rout_hbm.at[:, pl.ds(at, CW)], rw, 8),
        local(bias_hbm.at[:, pl.ds(at, CW)], bias, 9),
        local(alog_hbm.at[:, pl.ds(at, CW)], al, 10),
        local(skip_hbm.at[:, pl.ds(at, CW)], skip, 11),
    ]
    r = lax.axis_index("chan")
    zi = lax.div(r, 4)
    xi = lax.rem(r, 4)

    def chan(zz, xx):
        return 4 * lax.rem(zz + 12, 12) + lax.rem(xx + 4, 4)

    for one in (zbuf, zbuf_t, xbuf, xbuf_t):
        one[...] = jnp.zeros_like(one)
    barrier = pltpu.get_barrier_semaphore()
    for d in range(1, 12):
        @pl.when(zi + d < 12)
        def _():
            pl.semaphore_signal(barrier, inc=1, device_id={"chan": chan(zi + d, xi)}, device_id_type=MESH)
    for d in range(1, 4):
        @pl.when(xi + d < 4)
        def _():
            pl.semaphore_signal(barrier, inc=1, device_id={"chan": chan(zi, xi + d)}, device_id_type=MESH)
    for d in range(1, 16):
        pl.semaphore_signal(
            barrier, inc=1, device_id={"seq": lax.rem(s + d, 16)}, device_id_type=MESH
        )
    for one in loads:
        one.start()

    @pl.when(s < 1)
    def _():
        kb[1] = jnp.zeros_like(kb[1])
        vb[1] = jnp.zeros_like(vb[1])

    @pl.when(s < 2)
    def _():
        kb[2] = jnp.zeros_like(kb[2])
        vb[2] = jnp.zeros_like(vb[2])

    first = s * TOK
    qpos = first + lax.broadcasted_iota(jnp.int32, (TOK, TOK), 0)
    lane = lax.broadcasted_iota(jnp.int32, (TOK, TOK), 1)
    begin = jnp.zeros((TOK, TOK), jnp.int32)
    bound = jnp.int32(0)
    for j in range(16):
        bound = bound + doc[0, j]
        begin = jnp.where(qpos >= bound, bound, begin)
    masks = []
    for b in range(3):
        kpos = first - b * TOK + lane
        masks.append((kpos <= qpos) & (kpos >= begin))

    pl.semaphore_wait(barrier, 15 + zi + xi)
    for d in range(1, 4):
        @pl.when(xi - d >= 0)
        def _():
            pl.semaphore_signal(ready_x, inc=1, device_id={"chan": chan(zi, xi - d)}, device_id_type=MESH)
    for d in range(1, 12):
        @pl.when(zi - d >= 0)
        def _():
            pl.semaphore_signal(ready, inc=1, device_id={"chan": chan(zi - d, xi)}, device_id_type=MESH)

    def group(chip, i):
        off = jnp.int32(0)
        for at, value in enumerate(ORDER):
            off = jnp.where(i == at, value, off)
        return lax.rem(chip + off, 8)

    to1 = lax.rem(s + 1, 16)
    to2 = lax.rem(s + 2, 16)
    both = ((k_hbm.at[0], kb), (v_hbm.at[0], vb))

    def head(chip, i):
        return pl.ds(pl.multiple_of(group(chip, i) * 128, 128), 128)

    def send1(i):
        cols = head(lax.div(to1, 2), i)
        return [remote(o.at[:, cols], d.at[1, :, cols], kv_send.at[0, i, n], kv_recv.at[0, i, n], to1)
                for n, (o, d) in enumerate(both)]

    def send2(i):
        cols = head(lax.div(to2, 2), i)
        return [remote(o.at[:, cols], d.at[2, :, cols], kv_send.at[1, i, n], kv_recv.at[1, i, n], to2)
                for n, (o, d) in enumerate(both)]

    def pass2(i):
        cols = head(y, i)
        return [remote(d.at[1, :, cols], d.at[2, :, cols], kv_send.at[2, i, n], kv_recv.at[1, i, n], sib)
                for n, (o, d) in enumerate(both)]

    def start_kv(i, _):
        for n in range(2):
            @pl.when(s < 15)
            def _():
                send1(i)[n].start()

            @pl.when((c == 0) & (s < 14))
            def _():
                send2(i)[n].start()

        return 0

    lax.fori_loop(0, 8, start_kv, 0)

    def arrive_kv(i):
        cols = head(y, i)
        for n, (o, d) in enumerate(both):
            @pl.when(s >= 1)
            def _():
                remote(d.at[0, :, cols], d.at[1, :, cols], kv_send.at[0, i, n], kv_recv.at[0, i, n], sib).wait_recv()

            @pl.when((c == 0) & (s >= 2))
            def _():
                pass2(i)[n].start()

        for n, (o, d) in enumerate(both):
            @pl.when(s >= 2)
            def _():
                remote(d.at[0, :, cols], d.at[2, :, cols], kv_send.at[1, i, n], kv_recv.at[1, i, n], sib).wait_recv()

    for one in loads[:3]:
        one.wait()

    def send_tiles(g):
        for cc in range(2):
            to = 2 * g + cc
            cols = pl.ds(pl.multiple_of(to * CW, CW), CW)
            here = pl.ds(pl.multiple_of(s * TOK, TOK), TOK)

            @pl.when(to != s)
            def _():
                remote(ab.at[:, cols], x.at[here], x_send.at[to], x_recv.at[s], to).start()

            @pl.when(to == s)
            def _():
                local(ab.at[:, cols], x.at[here], 5).start()

    scale = LOG2E / math.sqrt(128.0)

    def step(i, _):
        arrive_kv(i)
        g = group(y, i)
        qcols = pl.ds(pl.multiple_of(g * 512, 512), 512)
        kcols = pl.ds(pl.multiple_of(g * 128, 128), 128)
        keys = [kb[b, :, kcols] for b in range(3)]
        vals = [vb[b, :, kcols] for b in range(3)]
        for j in range(4):
            hcols = pl.ds(pl.multiple_of(g * 512 + j * 128, 128), 128)
            q = qb[:, hcols]
            t = [jnp.where(masks[b], dot(q, keys[b], 1, 1) * scale, -1e30) for b in range(3)]
            top = jnp.max(jnp.maximum(jnp.maximum(t[0], t[1]), t[2]), axis=1, keepdims=True)
            e = [jnp.exp2(one - top) for one in t]
            inv = 1.0 / jnp.sum(e[0] + e[1] + e[2], axis=1, keepdims=True)
            o = dot((e[0] * inv).astype(BF16), vals[0])
            o = o + dot((e[1] * inv).astype(BF16), vals[1])
            o = o + dot((e[2] * inv).astype(BF16), vals[2])
            ab[:, hcols] = o.astype(BF16)

        @pl.when((i > 0) & (i < 7))
        def _():
            send_tiles(group(y, i - 1))

        return 0

    lax.fori_loop(0, 8, step, 0)
    out_copy = local(ab, attn_out.at[0], 6)
    out_copy.start()

    loads[3].wait()
    loads[4].wait()
    toks = ab[...]
    po[pl.ds(0, TOK), :] = dot(toks, wb[...]).astype(BF16)
    bct = dot(bb[...], toks, 1, 1)
    po[pl.ds(TOK, 2 * NS), :] = jnp.concatenate([bct, bct], axis=1).astype(BF16)

    own = local(po, pk.at[s], 7)
    own.start()

    def slot(chip, core):
        return 2 * lax.rem(chip + 8, 8) + core

    right = slot(y + 1, c)
    left = slot(y - 1, c)
    ring = {}
    across = {}
    across[0] = remote(po, pk.at[s], p_send.at[7], p_recv.at[s], sib)
    ring[("r", 0)] = remote(po, pk.at[s], p_send.at[0], p_recv.at[s], right)
    ring[("l", 0)] = remote(po, pk.at[s], p_send.at[4], p_recv.at[s], left)
    ring[("r", 0)].start()
    ring[("l", 0)].start()
    across[0].start()

    def relay(cc):
        to = 2 * lax.rem(y + 4, 8) + cc
        cols = pl.ds(pl.multiple_of(to * CW, CW), CW)
        return remote(ab.at[:, cols], rb.at[cc], r_send.at[cc], r_recv.at[cc], left)

    def forward(cc):
        frm = slot(y + 1, c)
        here = pl.ds(pl.multiple_of(frm * TOK, TOK), TOK)
        to = 2 * lax.rem(y + 5, 8) + cc
        return remote(rb.at[cc], x.at[here], f_send.at[cc], x_recv.at[frm], to)

    for cc in range(2):
        relay(cc).start()

    for one in loads[5:]:
        one.wait()
    rate = -jnp.exp(al[...]) * LOG2E
    rates = (rate[:8], rate[8:])

    row = lax.broadcasted_iota(jnp.int32, (TOK, TOK), 0)
    col = lax.broadcasted_iota(jnp.int32, (TOK, TOK), 1)
    tri = (col <= row).astype(BF16)
    spread = (lax.rem(lax.broadcasted_iota(jnp.int32, (NS, CW), 1), NS)
              == lax.broadcasted_iota(jnp.int32, (NS, CW), 0)).astype(BF16)
    block = (lax.div(lax.broadcasted_iota(jnp.int32, (TOK, CW), 1), NS)
             == lax.rem(lax.broadcasted_iota(jnp.int32, (TOK, CW), 0), NS))

    def prepare(*segs):
        for seg in segs:
            rows = pl.ds(pl.multiple_of(seg * TOK, TOK), TOK)
            low = pk[seg, pl.ds(0, TOK), :]
            step = softplus(dot(low, rw[...]) + bias[...])
            dt[rows, :] = step
            hi = step.astype(BF16)
            lo = (step - hi.astype(F32)).astype(BF16)
            run = dot(tri, hi) + dot(tri, lo)
            cum[rows, :] = run
            tot[pl.ds(seg, 1), :] = run[TOK - 1:, :]
            maps = pk[seg, pl.ds(TOK, 2 * NS), pl.ds(0, TOK)]
            bt[pl.ds(pl.multiple_of(seg * NS, NS), NS), :] = maps[:NS].astype(F32)
            wide_c = dot(maps[NS:], spread, 0, 0)
            cb[rows, :] = jnp.where(block, wide_c, 0.0).astype(BF16)

    def arrived(at):
        remote(po, pk.at[at], p_send.at[0], p_recv.at[at], sib).wait_recv()

    for k in range(1, 5):
        far = slot(y - k, c)
        arrived(far)
        if k < 4:
            ring[("r", k)] = remote(pk.at[far], pk.at[far], p_send.at[k], p_recv.at[far], right)
            ring[("r", k)].start()
        across[k] = remote(pk.at[far], pk.at[far], p_send.at[7 + k], p_recv.at[far], sib)
        across[k].start()
        if k < 4:
            far = slot(y + k, c)
            arrived(far)
            if k < 3:
                ring[("l", k)] = remote(pk.at[far], pk.at[far], p_send.at[4 + k], p_recv.at[far], left)
                ring[("l", k)].start()
            across[-k] = remote(pk.at[far], pk.at[far], p_send.at[11 + k], p_recv.at[far], sib)
            across[-k].start()
        if k == 1:
            send_tiles(group(y, 6))
            for cc in range(2):
                relay(cc).wait_recv()
                forward(cc).start()
            own.wait()
            arrived(slot(y, 1 - c))
            prepare(s, sib)
        elif k < 4:
            for far in (slot(y - k + 1, 1 - c), slot(y + k - 1, 1 - c)):
                arrived(far)
            prepare(slot(y - k + 1, c), slot(y + k - 1, c))
            prepare(slot(y - k + 1, 1 - c), slot(y + k - 1, 1 - c))

    for k in (-3, 3, 4):
        arrived(slot(y + k, 1 - c))
    prepare(slot(y - 3, c), slot(y + 3, c))
    prepare(slot(y - 3, 1 - c), slot(y + 3, 1 - c))
    prepare(slot(y + 4, c), slot(y + 4, 1 - c))

    def tile(of):
        return remote(
            ab.at[:, pl.ds(0, CW)], x.at[pl.ds(0, TOK)], x_send.at[of], x_recv.at[of], of
        )

    local(ab.at[:, pl.ds(0, CW)], x.at[pl.ds(0, TOK)], 5).wait()
    for d in range(1, 16):
        tile(lax.rem(s + d, 16)).wait_recv()

    def drive(seg, _):
        rows = pl.ds(pl.multiple_of(seg * TOK, TOK), TOK)
        u[rows, :] = dt[rows, :] * x[rows, :].astype(F32)
        return 0

    lax.fori_loop(0, SEGS, drive, 0)
    ha[...] = jnp.zeros_like(ha)
    hc[...] = jnp.zeros_like(hc)

    def rows_of(seg, chunk):
        return pl.ds(pl.multiple_of(seg * TOK + chunk * 16, 16), 16)

    def pair(p, _):
        def body(q, carry):
            states, maps = carry
            states = [list(one) for one in states]
            for half, (held, ready) in enumerate(((ha, hc), (hc, ha)) * 2):
                for k in range(PAR):
                    if half == 0:
                        wrapped = q == 0
                        seg = jnp.where(wrapped, lax.rem(p + 7, 8), p) * PAR + k
                        done = rows_of(seg, jnp.where(wrapped, 7, 4 * q - 1))
                    else:
                        done = rows_of(p * PAR + k, 4 * q + half - 1)
                    yl[done, :] = dot(cb[done, :], ready[k])
                for t in range(16):
                    for k in range(PAR):
                        near = pl.ds(pl.multiple_of((p * PAR + k) * TOK + q * 64, 64), 64)
                        lane = half * 16 + t
                        d = jnp.broadcast_to(dt.at[near][lane: lane + 1, :], (8, CW))
                        w = jnp.broadcast_to(u.at[near][lane: lane + 1, :], (8, CW))
                        for h in range(2):
                            b = jnp.broadcast_to(maps[k][8 * h: 8 * h + 8, lane: lane + 1], (8, TOK))
                            b = jnp.concatenate([b, b], axis=1)
                            states[k][h] = jnp.exp2(d * rates[h]) * states[k][h] + w * b
                        held[k, pl.ds(16 * t, 16), :] = jnp.concatenate(states[k], axis=0).astype(BF16)
            maps = tuple(pltpu.roll(one, TOK - 64, axis=1) for one in maps)
            return tuple(tuple(one) for one in states), maps

        zero = jnp.zeros((8, CW), F32)
        maps = tuple(
            bt[pl.ds(pl.multiple_of((p * PAR + k) * NS, NS), NS), :] for k in range(PAR)
        )
        states, _ = lax.fori_loop(0, 2, body, (((zero, zero),) * PAR, maps))
        for k in range(PAR):
            pre[p * PAR + k] = jnp.concatenate(states[k], axis=0)
        return 0

    lax.fori_loop(0, SEGS // PAR, pair, 0)
    for k in range(PAR):
        done = rows_of(SEGS - PAR + k, 7)
        yl[done, :] = dot(cb[done, :], hc[k])

    state = jnp.zeros((NS, CW), F32)
    total = jnp.zeros((1, CW), F32)
    for seg in range(SEGS):
        mine = pre[seg]
        t = tot[pl.ds(seg, 1), :]
        pre[seg] = state
        state = jnp.exp2(rate * t) * state + mine
        total = total + t
    pay[...] = state.astype(BF16)
    pay_t[...] = total

    def xcopy(d, slot):
        to = {"chan": chan(zi, xi + d)}
        return [pltpu.make_async_remote_copy(
            src_ref=o, dst_ref=i.at[slot], send_sem=xs_sem.at[d - 1, n], recv_sem=xr_sem.at[slot, n],
            device_id=to, device_id_type=MESH)
            for n, (o, i) in enumerate(((pay, xbuf), (pay_t, xbuf_t)))]

    @pl.when(xi < 3)
    def _():
        pl.semaphore_wait(ready_x, 3 - xi)

    for d in range(1, 4):
        for one in xcopy(d, xi):
            one.start()

    def decay(q, _):
        near = pl.ds(pl.multiple_of(TOK * q, TOK), TOK)
        for t in range(TOK):
            d = jnp.broadcast_to(cum.at[near][t: t + 1, :], (8, CW))
            e = [jnp.exp2(d * rates[h]).astype(BF16) for h in range(2)]
            held = pl.ds(pl.multiple_of(NS * TOK * q + 16 * t, 16), 16)
            ebuf[held, :] = jnp.concatenate(e, axis=0)
        return 0

    lax.fori_loop(0, EARLY, decay, 0)
    for d in range(1, 4):
        for one in xcopy(d, lax.rem(xi + d, 4)):
            one.wait_recv()
    gs = jnp.zeros((NS, CW), F32)
    gt = jnp.zeros((1, CW), F32)
    ms = jnp.zeros((NS, CW), F32)
    mt = jnp.zeros((1, CW), F32)
    for i in range(4):
        os = jnp.where(xi == i, state, xbuf[i].astype(F32))
        ot = jnp.where(xi == i, total, xbuf_t[i])
        dec = jnp.exp2(rate * ot)
        gs = dec * gs + os
        gt = gt + ot
        ms = jnp.where(i < xi, gs, ms)
        mt = jnp.where(i < xi, gt, mt)
    grp[...] = gs.astype(BF16)
    grp_t[...] = gt

    def zcopy(d, slot):
        to = {"chan": chan(zi + d, xi)}
        return [pltpu.make_async_remote_copy(
            src_ref=o, dst_ref=i.at[slot], send_sem=zs_sem.at[d, n], recv_sem=zr_sem.at[slot, n],
            device_id=to, device_id_type=MESH)
            for n, (o, i) in enumerate(((grp, zbuf), (grp_t, zbuf_t)))]


    @pl.when(zi < 11)
    def _():
        pl.semaphore_wait(ready, 11 - zi)

    for d in range(11, 0, -1):
        @pl.when(zi + d < 12)
        def _():
            for one in zcopy(d, zi):
                one.start()
    lax.fori_loop(EARLY, SEGS, decay, 0)
    for d in range(1, 12):
        @pl.when(zi - d >= 0)
        def _():
            for one in zcopy(d, lax.rem(zi - d + 12, 12)):
                one.wait_recv()
    zs = jnp.zeros((NS, CW), F32)
    for i in range(11):
        new = jnp.exp2(rate * zbuf_t[i]) * zs + zbuf[i].astype(F32)
        zs = jnp.where(i < zi, new, zs)
    row_in = jnp.exp2(rate * mt) * zs + ms
    done = jnp.zeros((1, CW), F32)
    for seg in range(SEGS):
        pre[seg] = pre[seg] + jnp.exp2(rate * done) * row_in
        done = done + tot[pl.ds(seg, 1), :]

    def carried(q, _):
        start = pre[q].astype(BF16)
        starts = jnp.concatenate([start] * 16, axis=0)
        for j in range(8):
            rows = pl.ds(pl.multiple_of(TOK * q + 16 * j, 16), 16)
            held = pl.ds(pl.multiple_of(NS * TOK * q + 256 * j, 256), 256)
            got = yl[rows, :] + dot(cb[rows, :], ebuf[held, :] * starts)
            out[0, rows, :] = (got + skip[...] * x[rows, :].astype(F32)).astype(BF16)
        return 0

    lax.fori_loop(0, SEGS, carried, 0)
    out_copy.wait()
    for one in list(ring.values()) + list(across.values()):
        one.wait_send()
    for cc in range(2):
        relay(cc).wait_send()
        forward(cc).wait_send()

    def end_kv(i, _):
        for n in range(2):
            @pl.when(s < 15)
            def _():
                send1(i)[n].wait_send()

            @pl.when((c == 0) & (s < 14))
            def _():
                send2(i)[n].wait_send()

            @pl.when((c == 0) & (s >= 2))
            def _():
                pass2(i)[n].wait_send()

        return 0

    lax.fori_loop(0, 8, end_kv, 0)
    for d in range(1, 16):
        to = lax.rem(s + d, 16)

        @pl.when(lax.rem(lax.div(to, 2) + 8 - y, 8) != 4)
        def _():
            tile(to).wait_send()

    for d in range(1, 4):
        for one in xcopy(d, xi):
            one.wait_send()
    for d in range(1, 12):
        @pl.when(zi + d < 12)
        def _():
            for one in zcopy(d, zi):
                one.wait_send()


def row(doc, queries, keys, values, rank_in, bc_weight, rank_out, dt_bias, a_log, skip_gain):
    anyspace = pl.BlockSpec(memory_space=pl.ANY)
    rows = SEGS * TOK
    return pl.pallas_call(
        row_kernel,
        out_shape=(
            jax.ShapeDtypeStruct((1, TOK, 4096), BF16),
            jax.ShapeDtypeStruct((1, rows, CW), BF16),
        ),
        in_specs=[pl.BlockSpec(memory_space=pltpu.SMEM)] + [anyspace] * 9,
        out_specs=(anyspace, pl.BlockSpec(memory_space=pltpu.VMEM)),
        scratch_shapes=[
            pltpu.VMEM((TOK, 4096), BF16),
            pltpu.VMEM((3, TOK, 1024), BF16),
            pltpu.VMEM((3, TOK, 1024), BF16),
            pltpu.VMEM((4096, 256), BF16),
            pltpu.VMEM((2 * NS, 4096), BF16),
            pltpu.VMEM((TOK, 4096), BF16),
            pltpu.VMEM((PACK, CW), BF16),
            pltpu.VMEM((2, TOK, CW), BF16),
            pltpu.VMEM((rows, CW), BF16),
            pltpu.VMEM((SEGS, PACK, CW), BF16),
            pltpu.VMEM((rows, CW), F32),
            pltpu.VMEM((rows, CW), F32),
            pltpu.VMEM((rows, CW), F32),
            pltpu.VMEM((rows, CW), BF16),
            pltpu.VMEM((rows, CW), F32),
            pltpu.VMEM((rows * NS, CW), BF16),
            pltpu.VMEM((SEGS, NS, CW), F32),
            pltpu.VMEM((PAR, 256, CW), BF16),
            pltpu.VMEM((PAR, 256, CW), BF16),
            pltpu.VMEM((256, CW), BF16),
            pltpu.VMEM((1, CW), F32),
            pltpu.VMEM((NS, CW), F32),
            pltpu.VMEM((1, CW), F32),
            pltpu.VMEM((SEGS * NS, TOK), F32),
            pltpu.VMEM((SEGS, CW), F32),
            pltpu.VMEM((NS, CW), BF16),
            pltpu.VMEM((1, CW), F32),
            pltpu.VMEM((NS, CW), BF16),
            pltpu.VMEM((1, CW), F32),
            pltpu.VMEM((4, NS, CW), BF16),
            pltpu.VMEM((4, 1, CW), F32),
            pltpu.VMEM((12, NS, CW), BF16),
            pltpu.VMEM((12, 1, CW), F32),
            pltpu.SemaphoreType.DMA((12,)),
            pltpu.SemaphoreType.DMA((3, 8, 2)),
            pltpu.SemaphoreType.DMA((2, 8, 2)),
            pltpu.SemaphoreType.DMA((16,)),
            pltpu.SemaphoreType.DMA((16,)),
            pltpu.SemaphoreType.DMA((15,)),
            pltpu.SemaphoreType.DMA((16,)),
            pltpu.SemaphoreType.DMA((2,)),
            pltpu.SemaphoreType.DMA((2,)),
            pltpu.SemaphoreType.DMA((2,)),
            pltpu.SemaphoreType.DMA((3, 2)),
            pltpu.SemaphoreType.DMA((4, 2)),
            pltpu.SemaphoreType.DMA((12, 2)),
            pltpu.SemaphoreType.DMA((12, 2)),
            pltpu.SemaphoreType.REGULAR,
            pltpu.SemaphoreType.REGULAR,
        ],
        compiler_params=pltpu.CompilerParams(
            collective_id=0, has_side_effects=True, vmem_limit_bytes=VMEM_LIMIT
        ),
        name="row",
    )(doc, queries, keys, values, rank_in, bc_weight, rank_out, dt_bias, a_log, skip_gain)


def local(
    queries, keys, values, doc_lengths, rank_in, bc_weight, rank_out, dt_bias, a_log, skip_gain
):
    return row(
        doc_lengths, queries, keys, values, rank_in, bc_weight.T,
        rank_out, dt_bias[None], a_log.T, skip_gain[None],
    )


def solution(mesh):
    return jax.shard_map(
        local,
        mesh=mesh,
        in_specs=(
            P("chan", "seq", None),
            P("chan", "seq", None),
            P("chan", "seq", None),
            P("chan", None),
            P(),
            P(),
            P(),
            P(),
            P(),
            P(),
        ),
        out_specs=(P("chan", "seq", None), P("chan", None, "seq")),
        check_vma=False,
    )
```
